256 devices in a mesh: row: 32 (over y, z), col: 8 (over x, core).
Axes of the slice: x: 4, y: 4, z: 8, core: 2. Of those that a mesh axis runs over, the one named last changes fastest.
Arguments:
- blocks: bfloat16 [4096, 3, 128, 128], P(('row', 'col')), may hold values from -0.3984375 to 0.3984375
- rows: int32 [4096, 3], P(('row', 'col')), may hold values from 0 to 63, as said below
- counts: int32 [4096], P(('row', 'col')), may hold values from 1 to 3
- sketch: bfloat16 [524288, 128], P(('row', 'col')), may hold values from -6 to 6
- weights: float32 [8192], replicated, may hold values from 0.35 to 2.8
Outputs:
- basis_out: float32 [8192, 128], P(('row', 'col'))
- right_factors: bfloat16 [524288, 128], P(('row', 'col'))
The draws below stay inside these ranges and needn't reach their ends.
Inputs may be any that keep to these rules, and one draw needn't show every extreme that they name: `rows`: the 3 entries of each document block are distinct feature blocks.
All inputs are finite; a program needn't handle non-finite values.
Results may differ from the reference program's by a relative error of at most 0.0049.
Values may be sent and summed in bfloat16 or wider, within the bound.
A program may use at most 64 MiB of HBM per device.

```python
import jax
import jax.numpy as jnp
from jax import lax

F = 8192
BLK = 128
L = 128
SLOTS = 3
POWER = 0
DB_DEV = 16
FB = 64
DOCB = 4096
DOCS = 524288


def draw_rows(key, part):
    row_keys = jax.random.split(jax.random.fold_in(key, 17), DOCB)

    def choose_rows(one_key):
        return jax.random.permutation(one_key, FB)[:SLOTS]
    return jax.vmap(choose_rows)(row_keys).astype(jnp.int32)


def draw_weights(key, part):
    position = jnp.arange(F, dtype=jnp.float32) / F
    trend = 0.6 * jnp.exp(jnp.log(3.0) * position)
    rough_key = jax.random.fold_in(key, 29)
    rough = jnp.exp(jax.random.uniform(rough_key, (F,), jnp.float32, jnp.log(0.7), jnp.log(1.4)))
    return (trend * rough).astype(jnp.float32)


def place_ends(entries, own_key, low, high):
    index_at = [jax.random.randint(jax.random.fold_in(own_key, axis), (), 0, length) for axis, length in enumerate(entries.shape)]
    longest = entries.shape.index(max(entries.shape))
    beside = index_at[:longest] + [(index_at[longest] + 1) % entries.shape[longest]] + index_at[longest + 1:]
    return entries.at[tuple(index_at)].set(low).at[tuple(beside)].set(high)


def block_levels(rng, shape, cuts, low, top_value):
    def one(dim, blocks):
        heights = jax.random.uniform(jax.random.fold_in(jax.random.fold_in(rng, 6), dim), (blocks,), jnp.float32, low / len(cuts), top_value / len(cuts))
        return jnp.repeat(jnp.exp(heights), shape[dim] // blocks).reshape((-1,) + (1,) * (len(shape) - dim - 1))

    gain = one(*cuts[0])
    for cut in cuts[1:]:
        gain = gain * one(*cut)
    return gain


def gaussian(own_key, extent, spread, limit, cuts=(), held_as=jnp.bfloat16):
    entries = jax.random.normal(own_key, extent, jnp.float32) * spread
    if len(cuts) > 0:
        entries = block_levels(own_key, extent, cuts, -0.22, 0.18) * entries
    return jnp.clip(entries, min=-limit, max=limit).astype(held_as)


def setup_inputs(seed: int = 0) -> dict:
    key_of = jax.random.split(jax.random.key(seed), 6)
    return {
        "blocks": gaussian(key_of[0], (DOCB, SLOTS, BLK, BLK), 0.0625, 0.3984375, ((0, 256),)),
        "rows": draw_rows(jax.random.fold_in(key_of[5], 71), 0),
        "counts": place_ends(jax.random.randint(key_of[2], (DOCB,), 1, SLOTS + 1), jax.random.fold_in(key_of[2], 1), 1, SLOTS).astype(jnp.int32),
        "sketch": gaussian(key_of[3], (DOCS, L), 1.0, 6.0, ((0, 256),)),
        "weights": draw_weights(jax.random.fold_in(key_of[5], 71), 0),
    }


def right_product(block_groups, id_groups, documents):
    groups = block_groups.shape[0]
    doc_groups = documents.reshape(groups, DB_DEV, BLK, L)

    def add_group(total, packed):
        tile_group, id_group, doc_group = packed
        terms = jnp.einsum('dsfk,dkl->dsfl', tile_group.astype(jnp.float32), doc_group.astype(jnp.float32), precision=lax.Precision.HIGHEST)
        summed = jax.ops.segment_sum(terms.reshape(DB_DEV * SLOTS, BLK, L), id_group, num_segments=FB + 1)
        return (total + summed, None)
    start_total = jnp.zeros((FB + 1, BLK, L), jnp.float32)
    total, _ = lax.scan(add_group, start_total, (block_groups, id_groups, doc_groups))
    return total[:FB].reshape(F, L)

def left_product(block_groups, row_groups, use_groups, weighted):
    weighted_blocks = weighted.reshape(FB, BLK, L)

    def one_group(packed):
        tile_group, row_group, use_group = packed
        picked = weighted_blocks[row_group].astype(jnp.float32)
        picked = jnp.where(use_group[:, :, None, None], picked, jnp.zeros((), jnp.float32))
        return jnp.einsum('dsfl,dsfk->dkl', picked, tile_group.astype(jnp.float32), precision=lax.Precision.HIGHEST)
    product = lax.map(one_group, (block_groups, row_groups, use_groups))
    return product.reshape(DOCS, L)

def normalize(summed):
    gram = jnp.dot(summed.T, summed, precision=lax.Precision.HIGHEST) / F
    chol_factor = jnp.linalg.cholesky(gram)
    inverse = jax.scipy.linalg.solve_triangular(chol_factor, jnp.eye(L, dtype=gram.dtype), lower=True)
    return jnp.dot(summed, inverse.T, precision=lax.Precision.HIGHEST)

def reference(blocks, rows, counts, sketch, weights):
    groups = DOCB // DB_DEV
    in_use = lax.broadcasted_iota(jnp.int32, (DOCB, SLOTS), 1) < counts[:, None]
    segment_ids = jnp.where(in_use, rows, FB).astype(jnp.int32)
    block_groups = blocks.reshape(groups, DB_DEV, SLOTS, BLK, BLK)
    id_groups = segment_ids.reshape(groups, DB_DEV * SLOTS)
    row_groups = rows.reshape(groups, DB_DEV, SLOTS)
    use_groups = in_use.reshape(groups, DB_DEV, SLOTS)
    scaling = weights[:, None]
    current = normalize(right_product(block_groups, id_groups, sketch) * scaling)
    for repeat in range(POWER):
        weighted = (current * scaling).astype(jnp.bfloat16)
        middle = left_product(block_groups, row_groups, use_groups, weighted).astype(jnp.bfloat16)
        current = normalize(right_product(block_groups, id_groups, middle) * scaling)
    weighted = (current * scaling).astype(jnp.bfloat16)
    factors = left_product(block_groups, row_groups, use_groups, weighted).astype(jnp.bfloat16)
    return (current, factors)
```

```python
import functools

import jax
import jax.numpy as jnp
from jax import lax
from jax.experimental import pallas as pl
from jax.experimental.pallas import tpu as pltpu
from jax.sharding import PartitionSpec as P

HIGHEST = lax.Precision.HIGHEST
MESH = pl.DeviceIdType.MESH
F32, BF16 = jnp.float32, jnp.bfloat16
NX, NY, NZ, NC = 4, 4, 8, 2
HZ = NZ // 2
PIECE = 32


def terms_kernel(rows_ref, counts_ref, blocks_ref, sketch_ref, acc_ref):
    docs, slots, width = blocks_ref.shape[:3]
    zero = jnp.zeros((8, width, width), F32)

    def clear(i, carry):
        acc_ref[pl.ds(i * 8, 8)] = zero
        return carry

    lax.fori_loop(0, acc_ref.shape[0] // 8, clear, 0)
    for d in range(docs):
        product = jnp.dot(
            blocks_ref[d].reshape(slots * width, width),
            sketch_ref[d * width : (d + 1) * width, :],
            preferred_element_type=F32,
        )
        for s in range(slots):
            part = product[s * width : (s + 1) * width]
            used = s < counts_ref[d]
            acc_ref[rows_ref[d, s]] += jnp.where(used, part, jnp.zeros_like(part))


def exchange_kernel(
    p_ref, w_ref, y_ref, s_ref,
    cs, cr, xs, xr, ys, yr, zs, zr, wide,
    sem0, sem_a, sem_b, sem_z, sem_gz, sem_gb, sem_ga, sem_p,
):
    row, col = lax.axis_index("row"), lax.axis_index("col")
    x, c = lax.div(col, NC), lax.rem(col, NC)
    y, z = lax.div(row, NZ), lax.rem(row, NZ)
    partner = (row, x * NC + (1 - c))

    def shift(v, k, n):
        return lax.rem(v + k, n)

    def at(xx, yy, zz):
        return (yy * NZ + zz, xx * NC + c)

    def x_peer(k):
        return at(shift(x, k, NX), y, z)

    def y_peer(k):
        return at(x, shift(y, k, NY), z)

    def z_peer(k):
        return at(x, y, shift(z, k, NZ))

    barrier = pltpu.get_barrier_semaphore()
    greet = [partner]
    greet += [x_peer(k) for k in range(1, NX)]
    greet += [y_peer(k) for k in range(1, NY)]
    greet += [z_peer(k) for k in range(1, NZ)]
    for peer in greet:
        pl.semaphore_signal(barrier, inc=1, device_id=peer, device_id_type=MESH)

    started = []

    def send(src, dst, sems, i, peer):
        copy = pltpu.make_async_remote_copy(
            src_ref=src, dst_ref=dst, send_sem=sems.at[0, i], recv_sem=sems.at[1, i],
            device_id=peer, device_id_type=MESH,
        )
        copy.start()
        started.append(copy)
        return copy

    def piece(colour, k, i, j, core):
        if colour == 0:
            return (i, j, shift(x, k, NX), core)
        return (shift(y, k, NY), HZ + j, i, core)

    order = [(q, k) for k in (1, 2, 3, 0) for q in (0, 1)]

    def slot(q, k):
        return q * 4 + k

    for q, k in order:
        def fill(i, carry, q=q, k=k):
            for j in range(HZ):
                cs[slot(q, k), i, j] = p_ref[piece(q, k, i, j, 1 - c)].astype(BF16)
            return carry

        lax.fori_loop(0, 4, fill, 0)

    flat = row * (NX * NC) + col
    w_row = w_ref[pl.ds(lax.div(flat, 4), 1), :]
    wide[...] = jnp.broadcast_to(w_row, wide.shape).T
    pl.semaphore_wait(barrier, len(greet))

    first = {}
    for q, k in order:
        n = slot(q, k)
        first[q, k] = send(cs.at[n], cr.at[n], sem0, n, partner)
    second = {}
    for q, k in order:
        first[q, k].wait_recv()
        if k == 0:
            continue
        n = q * 3 + k - 1

        def add(i, carry, q=q, k=k, n=n):
            for j in range(HZ):
                total = p_ref[piece(q, k, i, j, c)] + cr[slot(q, k), i, j].astype(F32)
                xs[n, i, j] = total.astype(BF16)
            return carry

        lax.fori_loop(0, 4, add, 0)
        second[q, k] = send(xs.at[n], xr.at[n], sem_a, n, (x_peer if q == 0 else y_peer)(k))

    third = {}
    for q in (0, 1):
        for k in (1, 2, 3):
            second[q, k].wait_recv()
        for k in (1, 2, 3, 0):
            i = shift(y if q == 0 else x, k, 4)
            for j in range(HZ):
                total = p_ref[piece(q, 0, i, j, c)] + cr[slot(q, 0), i, j].astype(F32)
                for m in range(3):
                    total = total + xr[q * 3 + m, i, j].astype(F32)
                if k > 0:
                    ys[q * 3 + k - 1, j] = total.astype(BF16)
                else:
                    zs[q * HZ + j] = total
            if k > 0:
                n = q * 3 + k - 1
                third[q, k] = send(ys.at[n], yr.at[n], sem_b, n, (y_peer if q == 0 else x_peer)(k))

    for q in (0, 1):
        for k in (1, 2, 3):
            third[q, k].wait_recv()
        for j in range(HZ):
            total = zs[q * HZ + j]
            for m in range(3):
                total = total + yr[q * 3 + m, j].astype(F32)
            zs[q * HZ + j] = total

    fourth = [
        send(zs.at[shift(z, k, NZ)], zr.at[k - 1], sem_z, k - 1, z_peer(k)) for k in range(1, NZ)
    ]
    total = zs[z]
    for k in range(1, NZ):
        fourth[k - 1].wait_recv()
        total = total + zr[k - 1]
    w = wide[pl.ds(pl.multiple_of(lax.rem(flat, 4) * PIECE, PIECE), PIECE), :]
    summed = total * w
    s_ref[...] = summed
    y_ref[y, z, x, c] = (summed * w).astype(BF16)

    mine = y_ref.at[y, z, x, c]
    gz = [send(mine, mine, sem_gz, k - 1, z_peer(k)) for k in range(1, NZ)]
    paired = []

    def pair(part):
        paired.append(send(part, part, sem_p, len(paired), partner))

    for copy in gz:
        copy.wait_recv()
    gb = {}
    for q in (0, 1):
        part = y_ref.at[y, pl.ds(q * HZ, HZ), x, c]
        for k in (1, 2, 3):
            gb[q, k] = send(part, part, sem_gb, q * 3 + k - 1, (y_peer if q == 0 else x_peer)(k))
    pair(y_ref.at[y, :, x, c])
    ga = {}
    for q in (0, 1):
        for k in (1, 2, 3):
            gb[q, k].wait_recv()
        part = y_ref.at[:, pl.ds(0, HZ), x, c] if q == 0 else y_ref.at[y, pl.ds(HZ, HZ), :, c]
        for k in (1, 2, 3):
            ga[q, k] = send(part, part, sem_ga, q * 3 + k - 1, (x_peer if q == 0 else y_peer)(k))
        for k in (1, 2, 3):
            if q == 0:
                pair(y_ref.at[shift(y, k, NY), pl.ds(0, HZ), x, c])
            else:
                pair(y_ref.at[y, pl.ds(HZ, HZ), shift(x, k, NX), c])
    for k in (1, 3, 2):
        for q in (0, 1):
            ga[q, k].wait_recv()
            if q == 0:
                pair(y_ref.at[:, pl.ds(0, HZ), shift(x, NX - k, NX), c])
            else:
                pair(y_ref.at[shift(y, NY - k, NY), pl.ds(HZ, HZ), :, c])
    for copy in paired:
        copy.wait_recv()
    for copy in started:
        copy.wait_send()


def gram_kernel(rows_ref, counts_ref, y_ref, blocks_ref, w_ref, g_ref, t_ref, turned):
    docs, slots, width = blocks_ref.shape[:3]
    features = y_ref.shape[0] * width

    def one(f, carry):
        tile = y_ref[f]
        across = tile.astype(F32).T
        turned[f] = across.astype(BF16)
        w = w_ref[pl.ds(f, 1), :]
        scaled = (across * (1.0 / (w * w))).astype(BF16)
        return carry + jnp.dot(scaled, tile, preferred_element_type=F32)

    gram = lax.fori_loop(0, y_ref.shape[0], one, jnp.zeros((width, width), F32))
    g_ref[...] = gram / features
    for d in range(docs):
        total = jnp.zeros((width, width), F32)
        for s in range(slots):
            part = turned[rows_ref[d, s]]
            part = jnp.where(s < counts_ref[d], part, jnp.zeros_like(part))
            total = total + jnp.dot(part, blocks_ref[d, s], preferred_element_type=F32)
        t_ref[d] = total


def split(a):
    high = a.astype(BF16)
    return high, (a - high.astype(F32)).astype(BF16)


def finish_kernel(t_ref, inverse_ref, s_ref, basis_ref, factors_ref):
    docs, width = t_ref.shape[:2]
    inverse = inverse_ref[...]
    basis_ref[...] = lax.dot_general(
        s_ref[...], inverse, (((1,), (1,)), ((), ())), precision=HIGHEST, preferred_element_type=F32
    )
    high, low = split(inverse)
    for d in range(docs):
        t_high, t_low = split(t_ref[d])
        out = jnp.dot(high, t_high, preferred_element_type=F32)
        out = out + jnp.dot(high, t_low, preferred_element_type=F32)
        out = out + jnp.dot(low, t_high, preferred_element_type=F32)
        factors_ref[d * width : (d + 1) * width, :] = out.T.astype(BF16)


def vmem():
    return pl.BlockSpec(memory_space=pltpu.VMEM)


def smem():
    return pl.BlockSpec(memory_space=pltpu.SMEM)


def body(blocks, rows, counts, sketch, weights):
    docs, slots, width = blocks.shape[:3]
    features = weights.shape[0]
    feature_blocks = features // width
    columns = sketch.shape[1]
    square = (width, columns)
    params = functools.partial(pltpu.CompilerParams, vmem_limit_bytes=24 << 20)
    terms = pl.pallas_call(
        terms_kernel,
        name="terms",
        out_shape=jax.ShapeDtypeStruct((feature_blocks,) + square, F32),
        in_specs=[smem(), smem(), vmem(), vmem()],
        out_specs=vmem(),
        compiler_params=params(),
    )(rows, counts, blocks, sketch)
    w = weights.reshape(feature_blocks, width)
    grid = (NY, NZ, NX, NC, PIECE, columns)
    tail = (PIECE, columns)
    dma = pltpu.SemaphoreType.DMA
    gathered, summed = pl.pallas_call(
        exchange_kernel,
        name="exchange",
        out_shape=(jax.ShapeDtypeStruct(grid, BF16), jax.ShapeDtypeStruct(tail, F32)),
        in_specs=[vmem(), vmem()],
        out_specs=(vmem(), vmem()),
        scratch_shapes=[
            pltpu.VMEM((8, 4, HZ) + tail, BF16), pltpu.VMEM((8, 4, HZ) + tail, BF16),
            pltpu.VMEM((6, 4, HZ) + tail, BF16), pltpu.VMEM((6, 4, HZ) + tail, BF16),
            pltpu.VMEM((6, HZ) + tail, BF16), pltpu.VMEM((6, HZ) + tail, BF16),
            pltpu.VMEM((NZ,) + tail, F32), pltpu.VMEM((NZ - 1,) + tail, F32),
            pltpu.VMEM(square, F32),
            dma((2, 8)), dma((2, 6)), dma((2, 6)), dma((2, NZ - 1)),
            dma((2, NZ - 1)), dma((2, 6)), dma((2, 6)), dma((2, 13)),
        ],
        compiler_params=params(collective_id=0, has_side_effects=True),
    )(terms.reshape(grid), w)
    gram, turned = pl.pallas_call(
        gram_kernel,
        name="gram",
        out_shape=(jax.ShapeDtypeStruct(square, F32), jax.ShapeDtypeStruct((docs,) + square, F32)),
        in_specs=[smem(), smem(), vmem(), vmem(), vmem()],
        out_specs=(vmem(), vmem()),
        scratch_shapes=[pltpu.VMEM((feature_blocks,) + square, BF16)],
        compiler_params=params(),
    )(rows, counts, gathered.reshape((feature_blocks,) + square), blocks, w)
    chol_factor = jnp.linalg.cholesky(gram, symmetrize_input=False)
    inverse = jax.scipy.linalg.solve_triangular(
        chol_factor, jnp.eye(columns, dtype=F32), lower=True
    )
    return pl.pallas_call(
        finish_kernel,
        name="finish",
        out_shape=(
            jax.ShapeDtypeStruct(tail, F32),
            jax.ShapeDtypeStruct((docs * width, columns), BF16),
        ),
        in_specs=[vmem(), vmem(), vmem()],
        out_specs=(vmem(), vmem()),
        compiler_params=params(),
    )(turned, inverse, summed)


def solution(mesh):
    placed = (
        P(("row", "col"), None, None, None),
        P(("row", "col"), None),
        P(("row", "col")),
        P(("row", "col"), None),
        P(),
    )
    return jax.shard_map(
        body,
        mesh=mesh,
        in_specs=placed,
        out_specs=(P(("row", "col"), None), P(("row", "col"), None)),
        check_vma=False,
    )
```

```python
import functools

import jax
import jax.numpy as jnp
from jax import lax
from jax.experimental import pallas as pl
from jax.experimental.pallas import tpu as pltpu
from jax.sharding import PartitionSpec as P

HIGHEST = lax.Precision.HIGHEST
MESH = pl.DeviceIdType.MESH
F32, BF16 = jnp.float32, jnp.bfloat16
NX, NY, NZ, NC = 4, 4, 8, 2
HZ = NZ // 2
PIECE = 32


def scalars(rows_hbm, counts_hbm, rows_ref, counts_ref, sems):
    copies = [
        pltpu.make_async_copy(rows_hbm, rows_ref, sems.at[0]),
        pltpu.make_async_copy(counts_hbm, counts_ref, sems.at[1]),
    ]
    for copy in copies:
        copy.start()
    return copies


def terms_kernel(
    rows_hbm, counts_hbm, blocks_ref, sketch_ref, acc_ref,
    held, docs_held, sems, rows_ref, counts_ref, sem_i,
):
    docs, slots, width = held.shape[:3]
    step = 4
    indices = scalars(rows_hbm, counts_hbm, rows_ref, counts_ref, sem_i)
    copies = []
    for i in range(docs // step):
        a = pltpu.make_async_copy(sketch_ref.at[pl.ds(i * step * width, step * width)], docs_held.at[pl.ds(i * step * width, step * width)], sems.at[0, i])
        c = pltpu.make_async_copy(blocks_ref.at[pl.ds(i * step, step)], held.at[pl.ds(i * step, step)], sems.at[1, i])
        a.start()
        c.start()
        copies.append((a, c))
    zero = jnp.zeros((8, width, width), F32)

    def clear(i, carry):
        acc_ref[pl.ds(i * 8, 8)] = zero
        return carry

    lax.fori_loop(0, acc_ref.shape[0] // 8, clear, 0)
    for copy in indices:
        copy.wait()
    for d in range(docs):
        if d % step == 0:
            for copy in copies[d // step]:
                copy.wait()
        product = jnp.dot(
            held[d].reshape(slots * width, width),
            docs_held[d * width : (d + 1) * width, :],
            preferred_element_type=F32,
        )
        for s in range(slots):
            part = product[s * width : (s + 1) * width]
            used = s < counts_ref[d]
            acc_ref[rows_ref[s, d]] += jnp.where(used, part, jnp.zeros_like(part))


def exchange_kernel(
    p_ref, w_ref, y_ref, s_ref,
    cs, cr, xs, xr, ys, yr, zs, zr, wide,
    sem0, sem_a, sem_b, sem_z, sem_gz, sem_gb, sem_ga, sem_p,
):
    row, col = lax.axis_index("row"), lax.axis_index("col")
    x, c = lax.div(col, NC), lax.rem(col, NC)
    y, z = lax.div(row, NZ), lax.rem(row, NZ)
    partner = (row, x * NC + (1 - c))

    def shift(v, k, n):
        return lax.rem(v + k, n)

    def at(xx, yy, zz):
        return (yy * NZ + zz, xx * NC + c)

    def x_peer(k):
        return at(shift(x, k, NX), y, z)

    def y_peer(k):
        return at(x, shift(y, k, NY), z)

    def z_peer(k):
        return at(x, y, shift(z, k, NZ))

    barrier = pltpu.get_barrier_semaphore()
    greet = [partner]
    greet += [x_peer(k) for k in range(1, NX)]
    greet += [y_peer(k) for k in range(1, NY)]
    greet += [z_peer(k) for k in range(1, NZ)]
    for peer in greet:
        pl.semaphore_signal(barrier, inc=1, device_id=peer, device_id_type=MESH)

    started = []

    def send(src, dst, sems, i, peer):
        copy = pltpu.make_async_remote_copy(
            src_ref=src, dst_ref=dst, send_sem=sems.at[0, i], recv_sem=sems.at[1, i],
            device_id=peer, device_id_type=MESH,
        )
        copy.start()
        started.append(copy)
        return copy

    def piece(colour, k, i, j, core):
        if colour == 0:
            return (i, j, shift(x, k, NX), core)
        return (shift(y, k, NY), HZ + j, i, core)

    order = [(q, k) for k in (1, 2, 3, 0) for q in (0, 1)]

    def slot(q, k):
        return q * 4 + k

    for q, k in order:
        def fill(i, carry, q=q, k=k):
            for j in range(HZ):
                cs[slot(q, k), i, j] = p_ref[piece(q, k, i, j, 1 - c)].astype(BF16)
            return carry

        lax.fori_loop(0, 4, fill, 0)

    flat = row * (NX * NC) + col
    w_row = w_ref[pl.ds(lax.div(flat, 4), 1), :]
    wide[...] = jnp.broadcast_to(w_row, wide.shape).T
    pl.semaphore_wait(barrier, len(greet))

    first = {}
    for q, k in order:
        n = slot(q, k)
        first[q, k] = send(cs.at[n], cr.at[n], sem0, n, partner)
    second = {}
    for q, k in order:
        first[q, k].wait_recv()
        if k == 0:
            continue
        n = q * 3 + k - 1

        def add(i, carry, q=q, k=k, n=n):
            for j in range(HZ):
                total = p_ref[piece(q, k, i, j, c)] + cr[slot(q, k), i, j].astype(F32)
                xs[n, i, j] = total.astype(BF16)
            return carry

        lax.fori_loop(0, 4, add, 0)
        second[q, k] = send(xs.at[n], xr.at[n], sem_a, n, (x_peer if q == 0 else y_peer)(k))

    third = {}
    for q in (0, 1):
        for k in (1, 2, 3):
            second[q, k].wait_recv()
        for k in (1, 2, 3, 0):
            i = shift(y if q == 0 else x, k, 4)
            for j in range(HZ):
                total = p_ref[piece(q, 0, i, j, c)] + cr[slot(q, 0), i, j].astype(F32)
                for m in range(3):
                    total = total + xr[q * 3 + m, i, j].astype(F32)
                if k > 0:
                    ys[q * 3 + k - 1, j] = total.astype(BF16)
                else:
                    zs[q * HZ + j] = total
            if k > 0:
                n = q * 3 + k - 1
                third[q, k] = send(ys.at[n], yr.at[n], sem_b, n, (y_peer if q == 0 else x_peer)(k))

    for q in (0, 1):
        for k in (1, 2, 3):
            third[q, k].wait_recv()
        for j in range(HZ):
            total = zs[q * HZ + j]
            for m in range(3):
                total = total + yr[q * 3 + m, j].astype(F32)
            zs[q * HZ + j] = total

    fourth = [
        send(zs.at[shift(z, k, NZ)], zr.at[k - 1], sem_z, k - 1, z_peer(k)) for k in range(1, NZ)
    ]
    total = zs[z]
    for k in range(1, NZ):
        fourth[k - 1].wait_recv()
        total = total + zr[k - 1]
    w = wide[pl.ds(pl.multiple_of(lax.rem(flat, 4) * PIECE, PIECE), PIECE), :]
    summed = total * w
    s_ref[...] = summed
    y_ref[y, z, x, c] = (summed * w).astype(BF16)

    mine = y_ref.at[y, z, x, c]
    gz = [send(mine, mine, sem_gz, k - 1, z_peer(k)) for k in range(1, NZ)]
    paired = []

    def pair(part):
        paired.append(send(part, part, sem_p, len(paired), partner))

    for copy in gz:
        copy.wait_recv()
    gb = {}
    for q in (0, 1):
        part = y_ref.at[y, pl.ds(q * HZ, HZ), x, c]
        for k in (1, 2, 3):
            gb[q, k] = send(part, part, sem_gb, q * 3 + k - 1, (y_peer if q == 0 else x_peer)(k))
    pair(y_ref.at[y, :, x, c])
    ga = {}
    for q in (0, 1):
        for k in (1, 2, 3):
            gb[q, k].wait_recv()
        part = y_ref.at[:, pl.ds(0, HZ), x, c] if q == 0 else y_ref.at[y, pl.ds(HZ, HZ), :, c]
        for k in (1, 2, 3):
            ga[q, k] = send(part, part, sem_ga, q * 3 + k - 1, (x_peer if q == 0 else y_peer)(k))
        for k in (1, 2, 3):
            if q == 0:
                pair(y_ref.at[shift(y, k, NY), pl.ds(0, HZ), x, c])
            else:
                pair(y_ref.at[y, pl.ds(HZ, HZ), shift(x, k, NX), c])
    for k in (1, 3, 2):
        for q in (0, 1):
            ga[q, k].wait_recv()
            if q == 0:
                pair(y_ref.at[:, pl.ds(0, HZ), shift(x, NX - k, NX), c])
            else:
                pair(y_ref.at[shift(y, NY - k, NY), pl.ds(HZ, HZ), :, c])
    for copy in paired:
        copy.wait_recv()
    for copy in started:
        copy.wait_send()


def split(a):
    high = a.astype(BF16)
    return high, (a - high.astype(F32)).astype(BF16)


def factor(m_ref, linv_ref, b):
    n = m_ref.shape[0]
    lane = lax.broadcasted_iota(jnp.int32, (b, n), 1)
    sub = lax.broadcasted_iota(jnp.int32, (b, n), 0)
    for r0 in range(0, n, b):
        panel = m_ref[r0 : r0 + b, :]
        cols = jnp.stack([jnp.broadcast_to(panel[:, r0 + j : r0 + j + 1], (b, n)) for j in range(b)])
        inside = (lane >= r0) & (lane < r0 + b)
        panel = jnp.where(inside, (lane - r0 == sub).astype(F32), panel)
        pivots = jnp.ones((b, n), F32)
        for k in range(b):
            base = (k // 8) * 8
            col = cols[0]
            pivot = col[k - base : k - base + 1]
            pivots = jnp.where(sub == k, pivot, pivots)
            if k == b - 1:
                break
            inv = 1.0 / pivot
            col = jnp.where(sub[base:] > k, col, 0.0)
            row = panel[k : k + 1] * inv
            lower = panel[base:] - col * row
            panel = lower if base == 0 else jnp.concatenate([panel[:base], lower], axis=0)
            rest = cols[1:]
            cols = rest - col[None] * (rest[:, k - base : k - base + 1, :] * inv)
            if (k + 1) % 8 == 0:
                cols = cols[:, 8:]
        scaled = panel * lax.rsqrt(pivots)
        linv_ref[r0 : r0 + b, :] = jnp.where(lane < r0 + b, scaled, 0.0)
        if r0 + b < n:
            h = scaled.astype(BF16)
            rem = scaled - h.astype(F32)
            m = rem.astype(BF16)
            l = (rem - m.astype(F32)).astype(BF16)
            right = lane >= r0 + b
            zero = jnp.zeros_like(h)
            hf, mf, lf = (jnp.where(right, v.astype(F32), 0.0).astype(BF16) for v in (h, m, l))
            left = jnp.concatenate([hf, hf, mf, mf, hf, lf], axis=0)
            rightm = jnp.concatenate([h, m, h, m, l, h], axis=0)
            update = lax.dot_general(left, rightm, (((0,), (0,)), ((), ())), preferred_element_type=F32)
            rest = m_ref[r0 + b :, :]
            lane2 = lax.broadcasted_iota(jnp.int32, rest.shape, 1)
            rest = jnp.where((lane2 >= r0) & (lane2 < r0 + b), 0.0, rest)
            m_ref[r0 + b :, :] = rest - update[r0 + b :, :]


def tail_kernel(
    rows_hbm, counts_hbm, y_ref, blocks_ref, w_ref, s_ref, basis_ref, factors_ref,
    turned, m_ref, linv_ref, t_ref, held, sem, rows_ref, counts_ref, sem_i,
):
    slots, docs = rows_ref.shape
    indices = scalars(rows_hbm, counts_hbm, rows_ref, counts_ref, sem_i)
    width = y_ref.shape[1]
    count = y_ref.shape[0]
    features = count * width
    copy = pltpu.make_async_copy(blocks_ref, held, sem)
    copy.start()
    group = 8

    def some(i, carry):
        scaled = []
        for j in range(group):
            f = i * group + j
            tile = y_ref[f]
            across = tile.T
            turned[f] = across
            w = w_ref[pl.ds(f, 1), :]
            scaled.append((across.astype(F32) * (1.0 / (w * w))).astype(BF16))
        left = jnp.concatenate(scaled, axis=1)
        right = y_ref[pl.ds(i * group, group)].reshape(group * width, width)
        return carry + jnp.dot(left, right, preferred_element_type=F32)

    gram = lax.fori_loop(0, count // group, some, jnp.zeros((width, width), F32))
    m_ref[...] = gram / features
    copy.wait()
    for copy in indices:
        copy.wait()

    def product(d):
        parts = []
        for s in range(slots):
            part = turned[rows_ref[s, d]]
            parts.append(jnp.where(s < counts_ref[d], part, jnp.zeros_like(part)))
        left = jnp.concatenate(parts, axis=1)
        right = held[d].reshape(slots * width, width)
        t_ref[d] = jnp.dot(left, right, preferred_element_type=F32)

    for d in range(docs):
        product(d)
    factor(m_ref, linv_ref, 16)
    inverse = linv_ref[...]
    basis_ref[...] = lax.dot_general(
        s_ref[...], inverse, (((1,), (1,)), ((), ())), precision=HIGHEST, preferred_element_type=F32
    )
    high, low = split(inverse)
    both = jnp.concatenate([high, high, low], axis=1)
    for d in range(docs):
        t_high, t_low = split(t_ref[d])
        out = jnp.dot(both, jnp.concatenate([t_high, t_low, t_high], axis=0), preferred_element_type=F32)
        factors_ref[d * width : (d + 1) * width, :] = out.T.astype(BF16)


def vmem():
    return pl.BlockSpec(memory_space=pltpu.VMEM)


def hbm():
    return pl.BlockSpec(memory_space=pltpu.HBM)


def body(blocks, rows, counts, sketch, weights):
    docs, slots, width = blocks.shape[:3]
    features = weights.shape[0]
    feature_blocks = features // width
    columns = sketch.shape[1]
    square = (width, columns)
    tail = (PIECE, columns)
    dma = pltpu.SemaphoreType.DMA
    params = functools.partial(pltpu.CompilerParams, vmem_limit_bytes=24 << 20)
    rows = rows.T
    rows, counts, blocks, sketch = (
        pltpu.with_memory_space_constraint(a, pltpu.HBM) for a in (rows, counts, blocks, sketch)
    )
    terms = pl.pallas_call(
        terms_kernel,
        name="terms",
        out_shape=jax.ShapeDtypeStruct((feature_blocks,) + square, F32),
        in_specs=[hbm()] * 4,
        out_specs=vmem(),
        scratch_shapes=[
            pltpu.VMEM(blocks.shape, BF16), pltpu.VMEM(sketch.shape, BF16), dma((2, 4)),
            pltpu.SMEM(rows.shape, jnp.int32), pltpu.SMEM(counts.shape, jnp.int32), dma((2,)),
        ],
        compiler_params=params(),
    )(rows, counts, blocks, sketch)
    w = weights.reshape(feature_blocks, width)
    grid = (NY, NZ, NX, NC, PIECE, columns)
    gathered, summed = pl.pallas_call(
        exchange_kernel,
        name="exchange",
        out_shape=(jax.ShapeDtypeStruct(grid, BF16), jax.ShapeDtypeStruct(tail, F32)),
        in_specs=[vmem(), vmem()],
        out_specs=(vmem(), vmem()),
        scratch_shapes=[
            pltpu.VMEM((8, 4, HZ) + tail, BF16), pltpu.VMEM((8, 4, HZ) + tail, BF16),
            pltpu.VMEM((6, 4, HZ) + tail, BF16), pltpu.VMEM((6, 4, HZ) + tail, BF16),
            pltpu.VMEM((6, HZ) + tail, BF16), pltpu.VMEM((6, HZ) + tail, BF16),
            pltpu.VMEM((NZ,) + tail, F32), pltpu.VMEM((NZ - 1,) + tail, F32),
            pltpu.VMEM(square, F32),
            dma((2, 8)), dma((2, 6)), dma((2, 6)), dma((2, NZ - 1)),
            dma((2, NZ - 1)), dma((2, 6)), dma((2, 6)), dma((2, 13)),
        ],
        compiler_params=params(collective_id=0, has_side_effects=True),
    )(terms.reshape(grid), w)
    return pl.pallas_call(
        tail_kernel,
        name="tail",
        out_shape=(
            jax.ShapeDtypeStruct(tail, F32),
            jax.ShapeDtypeStruct((docs * width, columns), BF16),
        ),
        in_specs=[hbm(), hbm(), vmem(), hbm(), vmem(), vmem()],
        out_specs=(vmem(), vmem()),
        scratch_shapes=[
            pltpu.VMEM((feature_blocks,) + square, BF16),
            pltpu.VMEM(square, F32), pltpu.VMEM(square, F32),
            pltpu.VMEM((docs,) + square, F32),
            pltpu.VMEM(blocks.shape, BF16), dma(()),
            pltpu.SMEM(rows.shape, jnp.int32), pltpu.SMEM(counts.shape, jnp.int32), dma((2,)),
        ],
        compiler_params=params(),
    )(rows, counts, gathered.reshape((feature_blocks,) + square), blocks, w, summed)


def solution(mesh):
    placed = (
        P(("row", "col"), None, None, None),
        P(("row", "col"), None),
        P(("row", "col")),
        P(("row", "col"), None),
        P(),
    )
    return jax.shard_map(
        body,
        mesh=mesh,
        in_specs=placed,
        out_specs=(P(("row", "col"), None), P(("row", "col"), None)),
        check_vma=False,
    )
```

```python
import functools

import jax
import jax.numpy as jnp
from jax import lax
from jax.experimental import pallas as pl
from jax.experimental.pallas import tpu as pltpu
from jax.sharding import PartitionSpec as P

HIGHEST = lax.Precision.HIGHEST
MESH = pl.DeviceIdType.MESH
F32, BF16 = jnp.float32, jnp.bfloat16
NX, NY, NZ, NC = 4, 4, 8, 2
QZ = 2
PIECE = 32


def scalars(rows_hbm, counts_hbm, rows_ref, counts_ref, sems):
    copies = [
        pltpu.make_async_copy(rows_hbm, rows_ref, sems.at[0]),
        pltpu.make_async_copy(counts_hbm, counts_ref, sems.at[1]),
    ]
    for copy in copies:
        copy.start()
    return copies


def terms_kernel(
    rows_hbm, counts_hbm, blocks_ref, sketch_ref, acc_ref,
    held, docs_held, sems, rows_ref, counts_ref, sem_i,
):
    docs, slots, width = held.shape[:3]
    step = 4
    indices = scalars(rows_hbm, counts_hbm, rows_ref, counts_ref, sem_i)
    copies = []
    for i in range(docs // step):
        a = pltpu.make_async_copy(sketch_ref.at[pl.ds(i * step * width, step * width)], docs_held.at[pl.ds(i * step * width, step * width)], sems.at[0, i])
        c = pltpu.make_async_copy(blocks_ref.at[pl.ds(i * step, step)], held.at[pl.ds(i * step, step)], sems.at[1, i])
        a.start()
        c.start()
        copies.append((a, c))
    zero = jnp.zeros((8, width, width), F32)

    def clear(i, carry):
        acc_ref[pl.ds(i * 8, 8)] = zero
        return carry

    lax.fori_loop(0, acc_ref.shape[0] // 8, clear, 0)
    for copy in indices:
        copy.wait()
    for d in range(docs):
        if d % step == 0:
            for copy in copies[d // step]:
                copy.wait()
        product = jnp.dot(
            held[d].reshape(slots * width, width),
            docs_held[d * width : (d + 1) * width, :],
            preferred_element_type=F32,
        )
        for s in range(slots):
            part = product[s * width : (s + 1) * width]
            used = s < counts_ref[d]
            acc_ref[rows_ref[s, d]] += jnp.where(used, part, jnp.zeros_like(part))


def exchange_kernel(
    p_ref, w_ref, y_ref, s_ref,
    cs, cr, xs, xr, ys, yr, zs, zr, wide,
    sem0, sem_a, sem_b, sem_z, sem_gz, sem_gb, sem_ga, sem_p,
):
    row, col = lax.axis_index("row"), lax.axis_index("col")
    x, c = lax.div(col, NC), lax.rem(col, NC)
    y, z = lax.div(row, NZ), lax.rem(row, NZ)
    partner = (row, x * NC + (1 - c))

    def shift(v, k, n):
        return lax.rem(v + k, n)

    def at(xx, yy, zz):
        return (yy * NZ + zz, xx * NC + c)

    x_peer = [at(shift(x, k, NX), y, z) for k in range(NX)]
    y_peer = [at(x, shift(y, k, NY), z) for k in range(NY)]
    z_peer = [at(x, y, shift(z, k, NZ)) for k in range(NZ)]
    greet = [partner] + z_peer[1:] + x_peer[1:] + y_peer[1:]
    barrier = pltpu.get_barrier_semaphore()
    for peer in greet:
        pl.semaphore_signal(barrier, inc=1, device_id=peer, device_id_type=MESH)

    streams = range(NZ // QZ)
    a_peer = [(x_peer, y_peer)[s % 2] for s in streams]
    b_peer = [(y_peer, x_peer)[s % 2] for s in streams]
    a_at = [(x, y)[s % 2] for s in streams]
    b_at = [(y, x)[s % 2] for s in streams]
    started = []

    def copy_to(src, dst, send_sem, recv_sem, peer):
        return pltpu.make_async_remote_copy(
            src_ref=src, dst_ref=dst, send_sem=send_sem, recv_sem=recv_sem,
            device_id=peer, device_id_type=MESH,
        )

    def send(src, dst, sems, i, peer):
        copy = copy_to(src, dst, sems.at[0, i], sems.at[1, i], peer)
        copy.start()
        started.append(copy)
        return copy

    def piece(s, k, b, j, core):
        a = shift(a_at[s], k, 4)
        if s % 2 == 0:
            return (b, s * QZ + j, a, core)
        return (a, s * QZ + j, b, core)

    order = [(s, k) for s0 in (0, 2) for k in (2, 1, 3, 0) for s in (s0, s0 + 1)]
    for s, k in order:
        def fill(b, carry, s=s, k=k):
            for j in range(QZ):
                cs[s * 4 + k, b, j] = p_ref[piece(s, k, b, j, 1 - c)].astype(BF16)
            return carry

        lax.fori_loop(0, 4, fill, 0)

    flat = row * (NX * NC) + col
    w_row = w_ref[pl.ds(lax.div(flat, 4), 1), :]
    wide[...] = jnp.broadcast_to(w_row, wide.shape).T
    pl.semaphore_wait(barrier, len(greet))

    first, second, third = {}, {}, {}
    for s, k in order:
        n = s * 4 + k
        first[s, k] = send(cs.at[n], cr.at[n], sem0, n, partner)
    for s, k in order:
        first[s, k].wait_recv()
        if k == 0:
            continue
        n = s * 3 + k - 1

        def add(b, carry, s=s, k=k, n=n):
            for j in range(QZ):
                total = p_ref[piece(s, k, b, j, c)] + cr[s * 4 + k, b, j].astype(F32)
                xs[n, b, j] = total.astype(BF16)
            return carry

        lax.fori_loop(0, 4, add, 0)
        second[s, k] = send(xs.at[n], xr.at[n], sem_a, n, a_peer[s][k])

    for s in streams:
        for k in (1, 3, 2):
            second[s, k].wait_recv()
        for k in (2, 1, 3, 0):
            b = shift(b_at[s], k, 4)
            for j in range(QZ):
                total = p_ref[piece(s, 0, b, j, c)] + cr[s * 4, b, j].astype(F32)
                for m in range(3):
                    total = total + xr[s * 3 + m, b, j].astype(F32)
                if k > 0:
                    ys[s * 3 + k - 1, j] = total.astype(BF16)
                else:
                    zs[s * QZ + j] = total
            if k > 0:
                n = s * 3 + k - 1
                third[s, k] = send(ys.at[n], yr.at[n], sem_b, n, b_peer[s][k])

    def fourth(there):
        return copy_to(
            zs.at[there], zr.at[z], sem_z.at[0, there], sem_z.at[1, z], at(x, y, there)
        )

    def arrival(k):
        here = shift(z, k, NZ)
        return copy_to(zs.at[here], zr.at[here], sem_z.at[0, here], sem_z.at[1, here], z_peer[k])

    for s in streams:
        for k in (1, 3, 2):
            third[s, k].wait_recv()
        for j in range(QZ):
            total = zs[s * QZ + j]
            for m in range(3):
                total = total + yr[s * 3 + m, j].astype(F32)
            zs[s * QZ + j] = total
        for j in range(QZ):
            there = s * QZ + j

            @pl.when(z != there)
            def _(there=there):
                fourth(there).start()

    total = zs[z]
    for k in (1, 7, 2, 6, 3, 5, 4):
        arrival(k).wait_recv()
        total = total + zr[shift(z, k, NZ)]
    w = wide[pl.ds(pl.multiple_of(lax.rem(flat, 4) * PIECE, PIECE), PIECE), :]
    summed = total * w
    s_ref[...] = summed

    mine_s, odd = lax.div(z, QZ), lax.rem(lax.div(z, QZ), 2)
    mine_a, mine_b = x + odd * (y - x), y + odd * (x - y)
    y_ref[mine_s, c, mine_a, mine_b, lax.rem(z, QZ)] = (summed * w).astype(BF16)
    mine = y_ref.at[mine_s, c, mine_a, mine_b, lax.rem(z, QZ)]
    for k in (4, 3, 5, 2, 6, 1, 7):
        copy = copy_to(mine, mine, sem_gz.at[0, k], sem_gz.at[1, z], z_peer[k])
        copy.start()
        started.append(copy)
    gb, ga, paired = {}, {}, []

    def pair(part):
        paired.append(send(part, part, sem_p, len(paired), partner))

    for s in streams:
        part = y_ref.at[s, c, a_at[s], b_at[s]]
        for j in range(QZ):
            there = s * QZ + j

            @pl.when(z != there)
            def _(there=there, j=j, part=part):
                copy_to(
                    part.at[j], part.at[j], sem_gz.at[0, 0], sem_gz.at[1, there], at(x, y, there)
                ).wait_recv()

        for k in (2, 1, 3):
            gb[s, k] = send(part, part, sem_gb, s * 3 + k - 1, b_peer[s][k])
    for s in streams:
        for k in (1, 3, 2):
            gb[s, k].wait_recv()
        part = y_ref.at[s, c, a_at[s]]
        for k in (2, 1, 3):
            ga[s, k] = send(part, part, sem_ga, s * 3 + k - 1, a_peer[s][k])
        pair(part)
    for s in streams:
        for k in (1, 3, 2):
            ga[s, k].wait_recv()
            pair(y_ref.at[s, c, shift(a_at[s], 4 - k, 4)])
    for copy in paired:
        copy.wait_recv()
    for copy in started:
        copy.wait_send()
    for k in range(1, NZ):
        arrival(k).wait_send()


def split(a):
    high = a.astype(BF16)
    return high, (a - high.astype(F32)).astype(BF16)


def factor(m_ref, linv_ref, b):
    n = m_ref.shape[0]
    lane = lax.broadcasted_iota(jnp.int32, (b, n), 1)
    sub = lax.broadcasted_iota(jnp.int32, (b, n), 0)
    for r0 in range(0, n, b):
        panel = m_ref[r0 : r0 + b, :]
        cols = jnp.stack([jnp.broadcast_to(panel[:, r0 + j : r0 + j + 1], (b, n)) for j in range(b)])
        inside = (lane >= r0) & (lane < r0 + b)
        panel = jnp.where(inside, (lane - r0 == sub).astype(F32), panel)
        pivots = jnp.ones((b, n), F32)
        for k in range(b):
            base = (k // 8) * 8
            col = cols[0]
            pivot = col[k - base : k - base + 1]
            pivots = jnp.where(sub == k, pivot, pivots)
            if k == b - 1:
                break
            inv = 1.0 / pivot
            col = jnp.where(sub[base:] > k, col, 0.0)
            row = panel[k : k + 1] * inv
            lower = panel[base:] - col * row
            panel = lower if base == 0 else jnp.concatenate([panel[:base], lower], axis=0)
            rest = cols[1:]
            cols = rest - col[None] * (rest[:, k - base : k - base + 1, :] * inv)
            if (k + 1) % 8 == 0:
                cols = cols[:, 8:]
        scaled = panel * lax.rsqrt(pivots)
        linv_ref[r0 : r0 + b, :] = jnp.where(lane < r0 + b, scaled, 0.0)
        if r0 + b < n:
            h = scaled.astype(BF16)
            rem = scaled - h.astype(F32)
            m = rem.astype(BF16)
            l = (rem - m.astype(F32)).astype(BF16)
            right = lane >= r0 + b
            zero = jnp.zeros_like(h)
            hf, mf, lf = (jnp.where(right, v.astype(F32), 0.0).astype(BF16) for v in (h, m, l))
            left = jnp.concatenate([hf, hf, mf, mf, hf, lf], axis=0)
            rightm = jnp.concatenate([h, m, h, m, l, h], axis=0)
            update = lax.dot_general(left, rightm, (((0,), (0,)), ((), ())), preferred_element_type=F32)
            rest = m_ref[r0 + b :, :]
            lane2 = lax.broadcasted_iota(jnp.int32, rest.shape, 1)
            rest = jnp.where((lane2 >= r0) & (lane2 < r0 + b), 0.0, rest)
            m_ref[r0 + b :, :] = rest - update[r0 + b :, :]


def tail_kernel(
    rows_hbm, counts_hbm, y_ref, blocks_ref, w_ref, s_ref, basis_ref, factors_ref,
    turned, m_ref, linv_ref, t_ref, held, sem, rows_ref, counts_ref, sem_i,
):
    slots, docs = rows_ref.shape
    indices = scalars(rows_hbm, counts_hbm, rows_ref, counts_ref, sem_i)
    count, width = w_ref.shape
    features = count * width
    copy = pltpu.make_async_copy(blocks_ref, held, sem)
    copy.start()
    group = 8

    def some(i, carry):
        scaled, tiles = [], []
        for j in range(group):
            f = i * group + j
            s, odd = lax.rem(i, 2) * 2 + j // 4, (j // 4) % 2
            tile = []
            for m in range(4):
                ax = (lax.div(i, 2), 2 * (j % 2) + m // 2)
                tile.append(y_ref[s, m % 2, ax[1 - odd], ax[odd], (j // 2) % 2])
            tile = jnp.concatenate(tile, axis=0)
            tiles.append(tile)
            across = tile.T
            turned[f] = across
            w = w_ref[pl.ds(f, 1), :]
            scaled.append((across.astype(F32) * (1.0 / (w * w))).astype(BF16))
        left = jnp.concatenate(scaled, axis=1)
        right = jnp.concatenate(tiles, axis=0)
        return carry + jnp.dot(left, right, preferred_element_type=F32)

    gram = lax.fori_loop(0, count // group, some, jnp.zeros((width, width), F32))
    m_ref[...] = gram / features
    copy.wait()
    for copy in indices:
        copy.wait()

    def product(d):
        parts = []
        for s in range(slots):
            part = turned[rows_ref[s, d]]
            parts.append(jnp.where(s < counts_ref[d], part, jnp.zeros_like(part)))
        left = jnp.concatenate(parts, axis=1)
        right = held[d].reshape(slots * width, width)
        t_ref[d] = jnp.dot(left, right, preferred_element_type=F32)

    for d in range(docs):
        product(d)
    factor(m_ref, linv_ref, 16)
    inverse = linv_ref[...]
    basis_ref[...] = lax.dot_general(
        s_ref[...], inverse, (((1,), (1,)), ((), ())), precision=HIGHEST, preferred_element_type=F32
    )
    high, low = split(inverse)
    both = jnp.concatenate([high, high, low], axis=1)
    for d in range(docs):
        t_high, t_low = split(t_ref[d])
        out = jnp.dot(both, jnp.concatenate([t_high, t_low, t_high], axis=0), preferred_element_type=F32)
        factors_ref[d * width : (d + 1) * width, :] = out.T.astype(BF16)


def vmem():
    return pl.BlockSpec(memory_space=pltpu.VMEM)


def hbm():
    return pl.BlockSpec(memory_space=pltpu.HBM)


def body(blocks, rows, counts, sketch, weights):
    docs, slots, width = blocks.shape[:3]
    features = weights.shape[0]
    feature_blocks = features // width
    columns = sketch.shape[1]
    square = (width, columns)
    tail = (PIECE, columns)
    dma = pltpu.SemaphoreType.DMA
    params = functools.partial(pltpu.CompilerParams, vmem_limit_bytes=24 << 20)
    rows = rows.T
    rows, counts, blocks, sketch = (
        pltpu.with_memory_space_constraint(a, pltpu.HBM) for a in (rows, counts, blocks, sketch)
    )
    terms = pl.pallas_call(
        terms_kernel,
        name="terms",
        out_shape=jax.ShapeDtypeStruct((feature_blocks,) + square, F32),
        in_specs=[hbm()] * 4,
        out_specs=vmem(),
        scratch_shapes=[
            pltpu.VMEM(blocks.shape, BF16), pltpu.VMEM(sketch.shape, BF16), dma((2, 4)),
            pltpu.SMEM(rows.shape, jnp.int32), pltpu.SMEM(counts.shape, jnp.int32), dma((2,)),
        ],
        compiler_params=params(),
    )(rows, counts, blocks, sketch)
    w = weights.reshape(feature_blocks, width)
    grid = (NY, NZ, NX, NC, PIECE, columns)
    streamed = (NZ // QZ, NC, 4, 4, QZ, PIECE, columns)
    gathered, summed = pl.pallas_call(
        exchange_kernel,
        name="exchange",
        out_shape=(jax.ShapeDtypeStruct(streamed, BF16), jax.ShapeDtypeStruct(tail, F32)),
        in_specs=[vmem(), vmem()],
        out_specs=(vmem(), vmem()),
        scratch_shapes=[
            pltpu.VMEM((16, 4, QZ) + tail, BF16), pltpu.VMEM((16, 4, QZ) + tail, BF16),
            pltpu.VMEM((12, 4, QZ) + tail, BF16), pltpu.VMEM((12, 4, QZ) + tail, BF16),
            pltpu.VMEM((12, QZ) + tail, BF16), pltpu.VMEM((12, QZ) + tail, BF16),
            pltpu.VMEM((NZ,) + tail, F32), pltpu.VMEM((NZ,) + tail, F32),
            pltpu.VMEM(square, F32),
            dma((2, 16)), dma((2, 12)), dma((2, 12)), dma((2, NZ)),
            dma((2, NZ)), dma((2, 12)), dma((2, 12)), dma((2, 16)),
        ],
        compiler_params=params(collective_id=0, has_side_effects=True),
    )(terms.reshape(grid), w)
    return pl.pallas_call(
        tail_kernel,
        name="tail",
        out_shape=(
            jax.ShapeDtypeStruct(tail, F32),
            jax.ShapeDtypeStruct((docs * width, columns), BF16),
        ),
        in_specs=[hbm(), hbm(), vmem(), hbm(), vmem(), vmem()],
        out_specs=(vmem(), vmem()),
        scratch_shapes=[
            pltpu.VMEM((feature_blocks,) + square, BF16),
            pltpu.VMEM(square, F32), pltpu.VMEM(square, F32),
            pltpu.VMEM((docs,) + square, F32),
            pltpu.VMEM(blocks.shape, BF16), dma(()),
            pltpu.SMEM(rows.shape, jnp.int32), pltpu.SMEM(counts.shape, jnp.int32), dma((2,)),
        ],
        compiler_params=params(),
    )(rows, counts, gathered, blocks, w, summed)


def solution(mesh):
    placed = (
        P(("row", "col"), None, None, None),
        P(("row", "col"), None),
        P(("row", "col")),
        P(("row", "col"), None),
        P(),
    )
    return jax.shard_map(
        body,
        mesh=mesh,
        in_specs=placed,
        out_specs=(P(("row", "col"), None), P(("row", "col"), None)),
        check_vma=False,
    )
```

```python
import functools

import jax
import jax.numpy as jnp
from jax import lax
from jax.experimental import pallas as pl
from jax.experimental.pallas import tpu as pltpu
from jax.sharding import PartitionSpec as P

HIGHEST = lax.Precision.HIGHEST
MESH = pl.DeviceIdType.MESH
F32, BF16 = jnp.float32, jnp.bfloat16
NX, NY, NZ, NC = 4, 4, 8, 2
QZ = 2
PIECE = 32


def scalars(rows_hbm, counts_hbm, rows_ref, counts_ref, sems):
    copies = [
        pltpu.make_async_copy(rows_hbm, rows_ref, sems.at[0]),
        pltpu.make_async_copy(counts_hbm, counts_ref, sems.at[1]),
    ]
    for copy in copies:
        copy.start()
    return copies


def terms_kernel(
    rows_hbm, counts_hbm, blocks_ref, sketch_ref, acc_ref,
    held, docs_held, sems, rows_ref, counts_ref, sem_i,
):
    docs, slots, width = held.shape[:3]
    step = 4
    indices = scalars(rows_hbm, counts_hbm, rows_ref, counts_ref, sem_i)
    copies = []
    for i in range(docs // step):
        a = pltpu.make_async_copy(sketch_ref.at[pl.ds(i * step * width, step * width)], docs_held.at[pl.ds(i * step * width, step * width)], sems.at[0, i])
        c = pltpu.make_async_copy(blocks_ref.at[pl.ds(i * step, step)], held.at[pl.ds(i * step, step)], sems.at[1, i])
        a.start()
        c.start()
        copies.append((a, c))
    zero = jnp.zeros((8, width, width), F32)

    def clear(i, carry):
        acc_ref[pl.ds(i * 8, 8)] = zero
        return carry

    lax.fori_loop(0, acc_ref.shape[0] // 8, clear, 0)
    for copy in indices:
        copy.wait()
    for d in range(docs):
        if d % step == 0:
            for copy in copies[d // step]:
                copy.wait()
        product = jnp.dot(
            held[d].reshape(slots * width, width),
            docs_held[d * width : (d + 1) * width, :],
            preferred_element_type=F32,
        )
        for s in range(slots):
            part = product[s * width : (s + 1) * width]
            used = s < counts_ref[d]
            acc_ref[rows_ref[s, d]] += jnp.where(used, part, jnp.zeros_like(part))


def exchange_kernel(
    p_ref, w_ref, blocks_ref, y_ref, s_ref, g_ref, bt_ref,
    held, sem_h, iw_ref, cs, cr, xs, xr, ys, yr, zs, zr, wide,
    sem0, sem_a, sem_b, sem_z, sem_gz, sem_gb, sem_ga, sem_p,
):
    row, col = lax.axis_index("row"), lax.axis_index("col")
    x, c = lax.div(col, NC), lax.rem(col, NC)
    y, z = lax.div(row, NZ), lax.rem(row, NZ)
    partner = (row, x * NC + (1 - c))

    def shift(v, k, n):
        return lax.rem(v + k, n)

    def at(xx, yy, zz):
        return (yy * NZ + zz, xx * NC + c)

    x_peer = [at(shift(x, k, NX), y, z) for k in range(NX)]
    y_peer = [at(x, shift(y, k, NY), z) for k in range(NY)]
    z_peer = [at(x, y, shift(z, k, NZ)) for k in range(NZ)]
    greet = [partner] + z_peer[1:] + x_peer[1:] + y_peer[1:]
    barrier = pltpu.get_barrier_semaphore()
    for peer in greet:
        pl.semaphore_signal(barrier, inc=1, device_id=peer, device_id_type=MESH)

    load = pltpu.make_async_copy(blocks_ref, held, sem_h)
    load.start()

    streams = range(NZ // QZ)
    a_peer = [(x_peer, y_peer)[s % 2] for s in streams]
    b_peer = [(y_peer, x_peer)[s % 2] for s in streams]
    a_at = [(x, y)[s % 2] for s in streams]
    b_at = [(y, x)[s % 2] for s in streams]
    started = []

    def copy_to(src, dst, send_sem, recv_sem, peer):
        return pltpu.make_async_remote_copy(
            src_ref=src, dst_ref=dst, send_sem=send_sem, recv_sem=recv_sem,
            device_id=peer, device_id_type=MESH,
        )

    def send(src, dst, sems, i, peer):
        copy = copy_to(src, dst, sems.at[0, i], sems.at[1, i], peer)
        copy.start()
        started.append(copy)
        return copy

    def piece(s, k, b, j, core):
        a = shift(a_at[s], k, 4)
        if s % 2 == 0:
            return (b, s * QZ + j, a, core)
        return (a, s * QZ + j, b, core)

    def inverse_weights(first, last):
        def some(i, carry):
            for j in range(8):
                w = w_ref[pl.ds(i * 8 + j, 1), :]
                turned = jnp.broadcast_to(1.0 / (w * w), wide.shape).T
                s, odd = lax.rem(i, 2) * 2 + j // 4, (j // 4) % 2
                for m in range(4):
                    ax = (lax.div(i, 2), 2 * (j % 2) + m // 2)
                    rows = turned[m * PIECE : (m + 1) * PIECE]
                    iw_ref[s, m % 2, ax[1 - odd], ax[odd], (j // 2) % 2] = rows
            return carry

        lax.fori_loop(first, last, some, 0)

    def turn_tiles(first, last):
        def some(i, carry):
            for j in range(4):
                d = i * 4 + j
                parts = [held[d, m].T for m in range(held.shape[1])]
                bt_ref[d] = jnp.concatenate(parts, axis=1)
            return carry

        lax.fori_loop(first, last, some, 0)

    def add_gram(s, core):
        tall = (4 * 4 * QZ * PIECE, wide.shape[1])
        part = y_ref[s, core].reshape(tall)
        scaled = (part.astype(F32) * iw_ref[s, core].reshape(tall)).astype(BF16)
        g_ref[...] += lax.dot_general(
            scaled, part, (((0,), (0,)), ((), ())), preferred_element_type=F32
        )

    order = [(s, k) for s0 in (0, 2) for k in (2, 1, 3, 0) for s in (s0, s0 + 1)]
    for s, k in order:
        def fill(b, carry, s=s, k=k):
            for j in range(QZ):
                cs[s * 4 + k, b, j] = p_ref[piece(s, k, b, j, 1 - c)].astype(BF16)
            return carry

        lax.fori_loop(0, 4, fill, 0)

    flat = row * (NX * NC) + col
    w_row = w_ref[pl.ds(lax.div(flat, 4), 1), :]
    wide[...] = jnp.broadcast_to(w_row, wide.shape).T
    pl.semaphore_wait(barrier, len(greet))

    first, second, third = {}, {}, {}
    for s, k in order:
        n = s * 4 + k
        first[s, k] = send(cs.at[n], cr.at[n], sem0, n, partner)
    for s, k in order:
        first[s, k].wait_recv()
        if k == 0:
            continue
        n = s * 3 + k - 1

        def add(b, carry, s=s, k=k, n=n):
            for j in range(QZ):
                total = p_ref[piece(s, k, b, j, c)] + cr[s * 4 + k, b, j].astype(F32)
                xs[n, b, j] = total.astype(BF16)
            return carry

        lax.fori_loop(0, 4, add, 0)
        second[s, k] = send(xs.at[n], xr.at[n], sem_a, n, a_peer[s][k])

    inverse_weights(0, 2)
    for s in streams:
        for k in (1, 3, 2):
            second[s, k].wait_recv()
        for k in (2, 1, 3, 0):
            b = shift(b_at[s], k, 4)
            for j in range(QZ):
                total = p_ref[piece(s, 0, b, j, c)] + cr[s * 4, b, j].astype(F32)
                for m in range(3):
                    total = total + xr[s * 3 + m, b, j].astype(F32)
                if k > 0:
                    ys[s * 3 + k - 1, j] = total.astype(BF16)
                else:
                    zs[s * QZ + j] = total
            if k > 0:
                n = s * 3 + k - 1
                third[s, k] = send(ys.at[n], yr.at[n], sem_b, n, b_peer[s][k])

    def fourth(there):
        return copy_to(
            zs.at[there], zr.at[z], sem_z.at[0, there], sem_z.at[1, z], at(x, y, there)
        )

    def arrival(k):
        here = shift(z, k, NZ)
        return copy_to(zs.at[here], zr.at[here], sem_z.at[0, here], sem_z.at[1, here], z_peer[k])

    for s in streams:
        for k in (1, 3, 2):
            third[s, k].wait_recv()
        for j in range(QZ):
            total = zs[s * QZ + j]
            for m in range(3):
                total = total + yr[s * 3 + m, j].astype(F32)
            zs[s * QZ + j] = total
        for j in range(QZ):
            there = s * QZ + j

            @pl.when(z != there)
            def _(there=there):
                fourth(there).start()

    inverse_weights(2, 6)
    total = zs[z]
    for k in (1, 7, 2, 6, 3, 5, 4):
        arrival(k).wait_recv()
        total = total + zr[shift(z, k, NZ)]
    w = wide[pl.ds(pl.multiple_of(lax.rem(flat, 4) * PIECE, PIECE), PIECE), :]
    summed = total * w
    s_ref[...] = summed

    mine_s, odd = lax.div(z, QZ), lax.rem(lax.div(z, QZ), 2)
    mine_a, mine_b = x + odd * (y - x), y + odd * (x - y)
    y_ref[mine_s, c, mine_a, mine_b, lax.rem(z, QZ)] = (summed * w).astype(BF16)
    mine = y_ref.at[mine_s, c, mine_a, mine_b, lax.rem(z, QZ)]
    for k in (4, 3, 5, 2, 6, 1, 7):
        copy = copy_to(mine, mine, sem_gz.at[0, k], sem_gz.at[1, z], z_peer[k])
        copy.start()
        started.append(copy)
    gb, ga, paired = {}, {}, []
    inverse_weights(6, 8)
    load.wait()
    turn_tiles(0, 4)
    g_ref[...] = jnp.zeros_like(g_ref)

    def pair(part):
        paired.append(send(part, part, sem_p, len(paired), partner))

    for s in streams:
        part = y_ref.at[s, c, a_at[s], b_at[s]]
        for j in range(QZ):
            there = s * QZ + j

            @pl.when(z != there)
            def _(there=there, j=j, part=part):
                copy_to(
                    part.at[j], part.at[j], sem_gz.at[0, 0], sem_gz.at[1, there], at(x, y, there)
                ).wait_recv()

        for k in (2, 1, 3):
            gb[s, k] = send(part, part, sem_gb, s * 3 + k - 1, b_peer[s][k])
    for s in streams:
        for k in (1, 3, 2):
            gb[s, k].wait_recv()
        part = y_ref.at[s, c, a_at[s]]
        for k in (2, 1, 3):
            ga[s, k] = send(part, part, sem_ga, s * 3 + k - 1, a_peer[s][k])
        pair(part)
    for s in streams:
        for k in (1, 3, 2):
            ga[s, k].wait_recv()
            pair(y_ref.at[s, c, shift(a_at[s], 4 - k, 4)])
        if s > 0:
            add_gram(s - 1, c)
    add_gram(streams[-1], c)
    for s in streams:
        for copy in [paired[s]] + paired[4 + 3 * s : 7 + 3 * s]:
            copy.wait_recv()
        add_gram(s, 1 - c)
    for copy in started:
        copy.wait_send()
    for k in range(1, NZ):
        arrival(k).wait_send()


def split(a):
    high = a.astype(BF16)
    return high, (a - high.astype(F32)).astype(BF16)


def factor(m_ref, linv_ref, b):
    n = m_ref.shape[0]
    whole = m_ref[...]
    on_diagonal = lax.broadcasted_iota(jnp.int32, (n, n), 0) == lax.broadcasted_iota(
        jnp.int32, (n, n), 1
    )
    diagonal = jnp.where(on_diagonal, whole, 0.0)
    across = lax.rsqrt(jnp.sum(diagonal, axis=0, keepdims=True))
    down = lax.rsqrt(jnp.sum(diagonal, axis=1, keepdims=True))
    m_ref[...] = whole * down * across
    lane = lax.broadcasted_iota(jnp.int32, (b, n), 1)
    sub = lax.broadcasted_iota(jnp.int32, (b, n), 0)
    for r0 in range(0, n, b):
        panel = m_ref[r0 : r0 + b, :]
        cols = jnp.stack(
            [jnp.broadcast_to(panel[:, r0 + j : r0 + j + 1], (b, n)) for j in range(b)]
        )
        inside = (lane >= r0) & (lane < r0 + b)
        panel = jnp.where(inside, (lane - r0 == sub).astype(F32), panel)
        pivots = jnp.ones((b, n), F32)
        for k in range(0, b, 2):
            base = (k // 8) * 8
            i = k - base
            c0, c1 = cols[0], cols[1]
            p, q, r = c0[i : i + 1], c1[i : i + 1], c1[i + 1 : i + 2]
            det = p * r - q * q
            over_p, over_det = 1.0 / p, 1.0 / det
            pivots = jnp.where(sub == k, p, jnp.where(sub == k + 1, det * over_p, pivots))
            below = sub[base:]
            alpha = jnp.where(
                below > k + 1,
                (r * c0 - q * c1) * over_det,
                jnp.where(below == k + 1, q * over_p, 0.0),
            )
            beta = jnp.where(below > k + 1, (p * c1 - q * c0) * over_det, 0.0)
            lower = panel[base:] - (alpha * panel[k : k + 1] + beta * panel[k + 1 : k + 2])
            panel = lower if base == 0 else jnp.concatenate([panel[:base], lower], axis=0)
            if k + 2 < b:
                rest = cols[2:]
                cols = rest - (
                    alpha[None] * rest[:, i : i + 1, :] + beta[None] * rest[:, i + 1 : i + 2, :]
                )
                if (k + 2) % 8 == 0:
                    cols = cols[:, 8:]
        scaled = panel * lax.rsqrt(pivots)
        linv_ref[r0 : r0 + b, :] = jnp.where(lane < r0 + b, scaled * across, 0.0)
        if r0 + b < n:
            h = scaled.astype(BF16)
            rem = scaled - h.astype(F32)
            m = rem.astype(BF16)
            l = (rem - m.astype(F32)).astype(BF16)
            right = lane >= r0 + b
            hf, mf, lf = (jnp.where(right, v.astype(F32), 0.0).astype(BF16) for v in (h, m, l))
            update = lax.dot_general(
                jnp.concatenate([hf, hf, mf, mf, hf, lf], axis=0),
                jnp.concatenate([h, m, h, m, l, h], axis=0),
                (((0,), (0,)), ((), ())),
                preferred_element_type=F32,
            )
            rest = m_ref[r0 + b :, :]
            lane2 = lax.broadcasted_iota(jnp.int32, rest.shape, 1)
            rest = jnp.where((lane2 >= r0) & (lane2 < r0 + b), 0.0, rest)
            m_ref[r0 + b :, :] = rest - update[r0 + b :, :]


def tail_kernel(
    rows_hbm, counts_hbm, y_ref, bt_ref, g_ref, s_ref, basis_ref, factors_ref,
    m_ref, linv_ref, t_ref, rows_ref, counts_ref, sem_i,
):
    slots, docs = rows_ref.shape
    width = g_ref.shape[0]
    features = y_ref.size // width
    indices = scalars(rows_hbm, counts_hbm, rows_ref, counts_ref, sem_i)
    m_ref[...] = g_ref[...] * (1.0 / features)
    for copy in indices:
        copy.wait()

    def tile(f):
        row = lax.div(f, 2)
        y, z = lax.div(row, NZ), lax.rem(row, NZ)
        s = lax.div(z, QZ)
        odd = lax.rem(s, 2)
        parts = []
        for m in range(4):
            x = lax.rem(f, 2) * 2 + m // 2
            a, b = x + odd * (y - x), y + odd * (x - y)
            parts.append(y_ref[s, m % 2, a, b, lax.rem(z, QZ)])
        return jnp.concatenate(parts, axis=0)

    for d in range(docs):
        parts = []
        for s in range(slots):
            part = tile(rows_ref[s, d])
            parts.append(jnp.where(s < counts_ref[d], part, jnp.zeros_like(part)))
        t_ref[d] = jnp.dot(bt_ref[d], jnp.concatenate(parts, axis=0), preferred_element_type=F32)
    factor(m_ref, linv_ref, 16)
    inverse = linv_ref[...]
    basis_ref[...] = lax.dot_general(
        s_ref[...], inverse, (((1,), (1,)), ((), ())), precision=HIGHEST, preferred_element_type=F32
    )
    high, low = split(inverse)
    both = jnp.concatenate([high, high, low], axis=1)
    for d in range(docs):
        t_high, t_low = split(t_ref[d])
        out = lax.dot_general(
            jnp.concatenate([t_high, t_low, t_high], axis=1), both,
            (((1,), (1,)), ((), ())), preferred_element_type=F32,
        )
        factors_ref[d * width : (d + 1) * width, :] = out.astype(BF16)


def vmem():
    return pl.BlockSpec(memory_space=pltpu.VMEM)


def hbm():
    return pl.BlockSpec(memory_space=pltpu.HBM)


def body(blocks, rows, counts, sketch, weights):
    docs, slots, width = blocks.shape[:3]
    features = weights.shape[0]
    feature_blocks = features // width
    columns = sketch.shape[1]
    square = (width, columns)
    tail = (PIECE, columns)
    dma = pltpu.SemaphoreType.DMA
    params = functools.partial(pltpu.CompilerParams, vmem_limit_bytes=24 << 20)
    rows = rows.T
    rows, counts, blocks, sketch = (
        pltpu.with_memory_space_constraint(a, pltpu.HBM) for a in (rows, counts, blocks, sketch)
    )
    terms = pl.pallas_call(
        terms_kernel,
        name="terms",
        out_shape=jax.ShapeDtypeStruct((feature_blocks,) + square, F32),
        in_specs=[hbm()] * 4,
        out_specs=vmem(),
        scratch_shapes=[
            pltpu.VMEM(blocks.shape, BF16), pltpu.VMEM(sketch.shape, BF16), dma((2, 4)),
            pltpu.SMEM(rows.shape, jnp.int32), pltpu.SMEM(counts.shape, jnp.int32), dma((2,)),
        ],
        compiler_params=params(),
    )(rows, counts, blocks, sketch)
    w = weights.reshape(feature_blocks, width)
    grid = (NY, NZ, NX, NC, PIECE, columns)
    streamed = (NZ // QZ, NC, 4, 4, QZ, PIECE, columns)
    gathered, summed, gram, turned = pl.pallas_call(
        exchange_kernel,
        name="exchange",
        out_shape=(
            jax.ShapeDtypeStruct(streamed, BF16), jax.ShapeDtypeStruct(tail, F32),
            jax.ShapeDtypeStruct(square, F32),
            jax.ShapeDtypeStruct((docs, width, slots * width), BF16),
        ),
        in_specs=[vmem(), vmem(), hbm()],
        out_specs=(vmem(), vmem(), vmem(), vmem()),
        scratch_shapes=[
            pltpu.VMEM(blocks.shape, BF16), dma(()), pltpu.VMEM(streamed, F32),
            pltpu.VMEM((16, 4, QZ) + tail, BF16), pltpu.VMEM((16, 4, QZ) + tail, BF16),
            pltpu.VMEM((12, 4, QZ) + tail, BF16), pltpu.VMEM((12, 4, QZ) + tail, BF16),
            pltpu.VMEM((12, QZ) + tail, BF16), pltpu.VMEM((12, QZ) + tail, BF16),
            pltpu.VMEM((NZ,) + tail, F32), pltpu.VMEM((NZ,) + tail, F32),
            pltpu.VMEM(square, F32),
            dma((2, 16)), dma((2, 12)), dma((2, 12)), dma((2, NZ)),
            dma((2, NZ)), dma((2, 12)), dma((2, 12)), dma((2, 16)),
        ],
        compiler_params=params(collective_id=0, has_side_effects=True),
    )(terms.reshape(grid), w, blocks)
    return pl.pallas_call(
        tail_kernel,
        name="tail",
        out_shape=(
            jax.ShapeDtypeStruct(tail, F32),
            jax.ShapeDtypeStruct((docs * width, columns), BF16),
        ),
        in_specs=[hbm(), hbm(), vmem(), vmem(), vmem(), vmem()],
        out_specs=(vmem(), vmem()),
        scratch_shapes=[
            pltpu.VMEM(square, F32), pltpu.VMEM(square, F32),
            pltpu.VMEM((docs,) + square, F32),
            pltpu.SMEM(rows.shape, jnp.int32), pltpu.SMEM(counts.shape, jnp.int32), dma((2,)),
        ],
        compiler_params=params(),
    )(rows, counts, gathered, turned, gram, summed)


def solution(mesh):
    placed = (
        P(("row", "col"), None, None, None),
        P(("row", "col"), None),
        P(("row", "col")),
        P(("row", "col"), None),
        P(),
    )
    return jax.shard_map(
        body,
        mesh=mesh,
        in_specs=placed,
        out_specs=(P(("row", "col"), None), P(("row", "col"), None)),
        check_vma=False,
    )
```

```python
import functools

import jax
import jax.numpy as jnp
from jax import lax
from jax.experimental import pallas as pl
from jax.experimental.pallas import tpu as pltpu
from jax.sharding import PartitionSpec as P

HIGHEST = lax.Precision.HIGHEST
MESH = pl.DeviceIdType.MESH
F32, BF16 = jnp.float32, jnp.bfloat16
NX, NY, NZ, NC = 4, 4, 8, 2
QZ = 2
PIECE = 32
PANEL = 16


def scalars(rows_hbm, counts_hbm, rows_ref, counts_ref, sems):
    copies = [
        pltpu.make_async_copy(rows_hbm, rows_ref, sems.at[0]),
        pltpu.make_async_copy(counts_hbm, counts_ref, sems.at[1]),
    ]
    for copy in copies:
        copy.start()
    return copies


def terms_kernel(
    rows_hbm, counts_hbm, blocks_ref, sketch_ref, acc_ref,
    held, docs_held, sems, rows_ref, counts_ref, sem_i,
):
    docs, slots, width = held.shape[:3]
    step = 4
    indices = scalars(rows_hbm, counts_hbm, rows_ref, counts_ref, sem_i)
    copies = []
    for i in range(docs // step):
        a = pltpu.make_async_copy(sketch_ref.at[pl.ds(i * step * width, step * width)], docs_held.at[pl.ds(i * step * width, step * width)], sems.at[0, i])
        c = pltpu.make_async_copy(blocks_ref.at[pl.ds(i * step, step)], held.at[pl.ds(i * step, step)], sems.at[1, i])
        a.start()
        c.start()
        copies.append((a, c))
    zero = jnp.zeros((8, width, width), F32)

    def clear(i, carry):
        acc_ref[pl.ds(i * 8, 8)] = zero
        return carry

    lax.fori_loop(0, acc_ref.shape[0] // 8, clear, 0)
    for copy in indices:
        copy.wait()
    for d in range(docs):
        if d % step == 0:
            for copy in copies[d // step]:
                copy.wait()
        product = jnp.dot(
            held[d].reshape(slots * width, width),
            docs_held[d * width : (d + 1) * width, :],
            preferred_element_type=F32,
        )
        for s in range(slots):
            part = product[s * width : (s + 1) * width]
            used = s < counts_ref[d]
            acc_ref[rows_ref[s, d]] += jnp.where(used, part, jnp.zeros_like(part))


def exchange_kernel(
    p_ref, w_ref, blocks_ref, y_ref, s_ref, g_ref, bt_ref,
    held, sem_h, iw_ref, cs, cr, xs, xr, ys, yr, zs, zr, wide,
    sem0, sem_a, sem_b, sem_z, sem_gz, sem_gb, sem_ga, sem_p,
):
    row, col = lax.axis_index("row"), lax.axis_index("col")
    x, c = lax.div(col, NC), lax.rem(col, NC)
    y, z = lax.div(row, NZ), lax.rem(row, NZ)
    partner = (row, x * NC + (1 - c))

    def shift(v, k, n):
        return lax.rem(v + k, n)

    def at(xx, yy, zz):
        return (yy * NZ + zz, xx * NC + c)

    x_peer = [at(shift(x, k, NX), y, z) for k in range(NX)]
    y_peer = [at(x, shift(y, k, NY), z) for k in range(NY)]
    z_peer = [at(x, y, shift(z, k, NZ)) for k in range(NZ)]
    greet = [z_peer[k] for k in (4, 3, 5, 2, 6)] + [x_peer[2], y_peer[2]]
    greet += [z_peer[1], z_peer[7], x_peer[1], x_peer[3], y_peer[1], y_peer[3], partner]
    barrier = pltpu.get_barrier_semaphore()
    for peer in greet:
        pl.semaphore_signal(barrier, inc=1, device_id=peer, device_id_type=MESH)

    load = pltpu.make_async_copy(blocks_ref, held, sem_h)
    load.start()

    streams = range(NZ // QZ)
    a_peer = [(x_peer, y_peer)[s % 2] for s in streams]
    b_peer = [(y_peer, x_peer)[s % 2] for s in streams]
    a_at = [(x, y)[s % 2] for s in streams]
    b_at = [(y, x)[s % 2] for s in streams]
    started = []

    def copy_to(src, dst, send_sem, recv_sem, peer):
        return pltpu.make_async_remote_copy(
            src_ref=src, dst_ref=dst, send_sem=send_sem, recv_sem=recv_sem,
            device_id=peer, device_id_type=MESH,
        )

    def send(src, dst, sems, i, peer):
        copy = copy_to(src, dst, sems.at[0, i], sems.at[1, i], peer)
        copy.start()
        started.append(copy)
        return copy

    def piece(s, k, b, j, core):
        a = shift(a_at[s], k, 4)
        if s % 2 == 0:
            return (b, s * QZ + j, a, core)
        return (a, s * QZ + j, b, core)

    def inverse_weights(first, last):
        def some(i, carry):
            for j in range(8):
                w = w_ref[pl.ds(i * 8 + j, 1), :]
                turned = jnp.broadcast_to(1.0 / (w * w), wide.shape).T
                s, odd = lax.rem(i, 2) * 2 + j // 4, (j // 4) % 2
                for m in range(4):
                    ax = (lax.div(i, 2), 2 * (j % 2) + m // 2)
                    rows = turned[m * PIECE : (m + 1) * PIECE]
                    iw_ref[s, m % 2, ax[1 - odd], ax[odd], (j // 2) % 2] = rows
            return carry

        lax.fori_loop(first, last, some, 0)

    def turn_tiles(first, last):
        def some(i, carry):
            for j in range(4):
                d = i * 4 + j
                parts = [held[d, m].T for m in range(held.shape[1])]
                bt_ref[d] = jnp.concatenate(parts, axis=1)
            return carry

        lax.fori_loop(first, last, some, 0)

    def add_gram(s, core):
        tall = (4 * 4 * QZ * PIECE, wide.shape[1])
        part = y_ref[s, core].reshape(tall)
        scaled = (part.astype(F32) * iw_ref[s, core].reshape(tall)).astype(BF16)
        g_ref[...] += lax.dot_general(
            scaled, part, (((0,), (0,)), ((), ())), preferred_element_type=F32
        )

    order = [(s, k) for s0 in (0, 2) for k in (2, 1, 3, 0) for s in (s0, s0 + 1)]
    for s, k in order:
        def fill(b, carry, s=s, k=k):
            for j in range(QZ):
                cs[s * 4 + k, b, j] = p_ref[piece(s, k, b, j, 1 - c)].astype(BF16)
            return carry

        lax.fori_loop(0, 4, fill, 0)

    flat = row * (NX * NC) + col
    w_row = w_ref[pl.ds(lax.div(flat, 4), 1), :]
    wide[...] = jnp.broadcast_to(w_row, wide.shape).T
    pl.semaphore_wait(barrier, len(greet))

    first, second, third = {}, {}, {}
    for s, k in order:
        n = s * 4 + k
        first[s, k] = send(cs.at[n], cr.at[n], sem0, n, partner)
    for s, k in order:
        first[s, k].wait_recv()
        if k == 0:
            continue
        n = s * 3 + k - 1

        def add(b, carry, s=s, k=k, n=n):
            for j in range(QZ):
                total = p_ref[piece(s, k, b, j, c)] + cr[s * 4 + k, b, j].astype(F32)
                xs[n, b, j] = total.astype(BF16)
            return carry

        lax.fori_loop(0, 4, add, 0)
        second[s, k] = send(xs.at[n], xr.at[n], sem_a, n, a_peer[s][k])

    inverse_weights(0, 2)
    for s in streams:
        for k in (1, 3, 2):
            second[s, k].wait_recv()
        for k in (2, 1, 3, 0):
            b = shift(b_at[s], k, 4)
            for j in range(QZ):
                total = p_ref[piece(s, 0, b, j, c)] + cr[s * 4, b, j].astype(F32)
                for m in range(3):
                    total = total + xr[s * 3 + m, b, j].astype(F32)
                if k > 0:
                    ys[s * 3 + k - 1, j] = total.astype(BF16)
                else:
                    zs[s * QZ + j] = total
            if k > 0:
                n = s * 3 + k - 1
                third[s, k] = send(ys.at[n], yr.at[n], sem_b, n, b_peer[s][k])

    def fourth(there):
        return copy_to(
            zs.at[there], zr.at[z], sem_z.at[0, there], sem_z.at[1, z], at(x, y, there)
        )

    def arrival(k):
        here = shift(z, k, NZ)
        return copy_to(zs.at[here], zr.at[here], sem_z.at[0, here], sem_z.at[1, here], z_peer[k])

    for s in streams:
        for k in (1, 3, 2):
            third[s, k].wait_recv()
        for j in range(QZ):
            total = zs[s * QZ + j]
            for m in range(3):
                total = total + yr[s * 3 + m, j].astype(F32)
            zs[s * QZ + j] = total
        for j in range(QZ):
            there = s * QZ + j

            @pl.when(z != there)
            def _(there=there):
                fourth(there).start()

    inverse_weights(2, 6)
    total = zs[z]
    for k in (1, 7, 2, 6, 3, 5, 4):
        arrival(k).wait_recv()
        total = total + zr[shift(z, k, NZ)]
    w = wide[pl.ds(pl.multiple_of(lax.rem(flat, 4) * PIECE, PIECE), PIECE), :]
    summed = total * w
    s_ref[...] = summed

    mine_s, odd = lax.div(z, QZ), lax.rem(lax.div(z, QZ), 2)
    mine_a, mine_b = x + odd * (y - x), y + odd * (x - y)
    y_ref[mine_s, c, mine_a, mine_b, lax.rem(z, QZ)] = (summed * w).astype(BF16)
    mine = y_ref.at[mine_s, c, mine_a, mine_b, lax.rem(z, QZ)]
    for k in (4, 3, 5, 2, 6, 1, 7):
        copy = copy_to(mine, mine, sem_gz.at[0, k], sem_gz.at[1, z], z_peer[k])
        copy.start()
        started.append(copy)
    gb, ga, paired = {}, {}, []
    inverse_weights(6, 8)
    load.wait()
    turn_tiles(0, 4)
    g_ref[...] = jnp.zeros_like(g_ref)

    def pair(part):
        paired.append(send(part, part, sem_p, len(paired), partner))

    for s in streams:
        part = y_ref.at[s, c, a_at[s], b_at[s]]
        for j in range(QZ):
            there = s * QZ + j

            @pl.when(z != there)
            def _(there=there, j=j, part=part):
                copy_to(
                    part.at[j], part.at[j], sem_gz.at[0, 0], sem_gz.at[1, there], at(x, y, there)
                ).wait_recv()

        for k in (2, 1, 3):
            gb[s, k] = send(part, part, sem_gb, s * 3 + k - 1, b_peer[s][k])
    for s in streams:
        for k in (1, 3, 2):
            gb[s, k].wait_recv()
        part = y_ref.at[s, c, a_at[s]]
        for k in (2, 1, 3):
            ga[s, k] = send(part, part, sem_ga, s * 3 + k - 1, a_peer[s][k])
        pair(part)
    def add_partner(s):
        for copy in [paired[s]] + paired[4 + 3 * s : 7 + 3 * s]:
            copy.wait_recv()
        add_gram(s, 1 - c)

    for s in streams:
        for k in (1, 3, 2):
            ga[s, k].wait_recv()
            pair(y_ref.at[s, c, shift(a_at[s], 4 - k, 4)])
        if s > 0:
            add_gram(s - 1, c)
        if s > 1:
            add_partner(s - 2)
    add_gram(streams[-1], c)
    for s in streams[-2:]:
        add_partner(s)
    for copy in started:
        copy.wait_send()
    for k in range(1, NZ):
        arrival(k).wait_send()


def split(a):
    high = a.astype(BF16)
    return high, (a - high.astype(F32)).astype(BF16)


def factor(m_ref, linv_ref, b, between):
    n = m_ref.shape[0]
    whole = m_ref[...]
    on_diagonal = lax.broadcasted_iota(jnp.int32, (n, n), 0) == lax.broadcasted_iota(
        jnp.int32, (n, n), 1
    )
    diagonal = jnp.where(on_diagonal, whole, 0.0)
    across = lax.rsqrt(jnp.sum(diagonal, axis=0, keepdims=True))
    down = lax.rsqrt(jnp.sum(diagonal, axis=1, keepdims=True))
    m_ref[...] = whole * down * across
    lane = lax.broadcasted_iota(jnp.int32, (b, n), 1)
    sub = lax.broadcasted_iota(jnp.int32, (b, n), 0)
    for r0 in range(0, n, b):
        panel = m_ref[r0 : r0 + b, :]
        cols = jnp.stack(
            [jnp.broadcast_to(panel[:, r0 + j : r0 + j + 1], (b, n)) for j in range(b)]
        )
        inside = (lane >= r0) & (lane < r0 + b)
        panel = jnp.where(inside, (lane - r0 == sub).astype(F32), panel)
        pivots = jnp.ones((b, n), F32)
        for k in range(0, b, 2):
            base = (k // 8) * 8
            i = k - base
            c0, c1 = cols[0], cols[1]
            p, q, r = c0[i : i + 1], c1[i : i + 1], c1[i + 1 : i + 2]
            det = p * r - q * q
            over_p, over_det = 1.0 / p, 1.0 / det
            pivots = jnp.where(sub == k, p, jnp.where(sub == k + 1, det * over_p, pivots))
            below = sub[base:]
            alpha = jnp.where(
                below > k + 1,
                (r * c0 - q * c1) * over_det,
                jnp.where(below == k + 1, q * over_p, 0.0),
            )
            beta = jnp.where(below > k + 1, (p * c1 - q * c0) * over_det, 0.0)
            lower = panel[base:] - (alpha * panel[k : k + 1] + beta * panel[k + 1 : k + 2])
            panel = lower if base == 0 else jnp.concatenate([panel[:base], lower], axis=0)
            if k + 2 < b:
                rest = cols[2:]
                cols = rest - (
                    alpha[None] * rest[:, i : i + 1, :] + beta[None] * rest[:, i + 1 : i + 2, :]
                )
                if (k + 2) % 8 == 0:
                    cols = cols[:, 8:]
        scaled = panel * lax.rsqrt(pivots)
        linv_ref[r0 : r0 + b, :] = jnp.where(lane < r0 + b, scaled * across, 0.0)
        if r0 + b < n:
            h = scaled.astype(BF16)
            rem = scaled - h.astype(F32)
            m = rem.astype(BF16)
            l = (rem - m.astype(F32)).astype(BF16)
            right = lane >= r0 + b
            hf, mf, lf = (jnp.where(right, v.astype(F32), 0.0).astype(BF16) for v in (h, m, l))
            update = lax.dot_general(
                jnp.concatenate([hf, hf, mf, mf, hf, lf], axis=0),
                jnp.concatenate([h, m, h, m, l, h], axis=0),
                (((0,), (0,)), ((), ())),
                preferred_element_type=F32,
            )
            rest = m_ref[r0 + b :, :]
            lane2 = lax.broadcasted_iota(jnp.int32, rest.shape, 1)
            rest = jnp.where((lane2 >= r0) & (lane2 < r0 + b), 0.0, rest)
            m_ref[r0 + b :, :] = rest - update[r0 + b :, :]
        between(r0 // b)


def tail_kernel(
    rows_hbm, counts_hbm, y_ref, bt_ref, g_ref, s_ref, basis_ref, factors_ref,
    m_ref, linv_ref, t_ref, f_ref, b_ref, sem_o, rows_ref, counts_ref, sem_i,
):
    slots, docs = rows_ref.shape
    width = g_ref.shape[0]
    features = y_ref.size // width
    indices = scalars(rows_hbm, counts_hbm, rows_ref, counts_ref, sem_i)
    m_ref[...] = g_ref[...] * (1.0 / features)

    def tile(f):
        row = lax.div(f, 2)
        y, z = lax.div(row, NZ), lax.rem(row, NZ)
        s = lax.div(z, QZ)
        odd = lax.rem(s, 2)
        parts = []
        for m in range(4):
            x = lax.rem(f, 2) * 2 + m // 2
            a, b = x + odd * (y - x), y + odd * (x - y)
            parts.append(y_ref[s, m % 2, a, b, lax.rem(z, QZ)])
        return jnp.concatenate(parts, axis=0)

    def product(d):
        parts = []
        for s in range(slots):
            part = tile(rows_ref[s, d])
            parts.append(jnp.where(s < counts_ref[d], part, jnp.zeros_like(part)))
        t_ref[d] = jnp.dot(bt_ref[d], jnp.concatenate(parts, axis=0), preferred_element_type=F32)

    panels = width // PANEL

    def between(panel):
        if panel == 0:
            for copy in indices:
                copy.wait()
        last = docs * (panel + 1) // panels
        for d in range(docs * panel // panels, last):
            product(d)

    factor(m_ref, linv_ref, PANEL, between)
    inverse = linv_ref[...]
    high, low = split(inverse)
    left = jnp.concatenate([high, low], axis=0)
    right = jnp.concatenate([high, jnp.zeros_like(low)], axis=0)
    both = jnp.concatenate([left, right], axis=1)
    copies = []

    def put(src, dst):
        copy = pltpu.make_async_copy(src, dst, sem_o.at[len(copies)])
        copy.start()
        copies.append(copy)

    for d in range(docs):
        t_high, t_low = split(t_ref[d])
        out = lax.dot_general(
            jnp.concatenate([t_high, t_low], axis=1), both,
            (((1,), (1,)), ((), ())), preferred_element_type=F32,
        )
        rows = pl.ds(d * width, width)
        f_ref[rows, :] = (out[:, :width] + out[:, width:]).astype(BF16)
        if d % 4 == 3:
            rows = pl.ds((d - 3) * width, 4 * width)
            put(f_ref.at[rows], factors_ref.at[rows])
        if d == 0:
            b_ref[...] = lax.dot_general(
                s_ref[...], inverse, (((1,), (1,)), ((), ())),
                precision=HIGHEST, preferred_element_type=F32,
            )
            put(b_ref, basis_ref)
    for copy in copies:
        copy.wait()


def vmem():
    return pl.BlockSpec(memory_space=pltpu.VMEM)


def hbm():
    return pl.BlockSpec(memory_space=pltpu.HBM)


def body(blocks, rows, counts, sketch, weights):
    docs, slots, width = blocks.shape[:3]
    features = weights.shape[0]
    feature_blocks = features // width
    columns = sketch.shape[1]
    square = (width, columns)
    tail = (PIECE, columns)
    dma = pltpu.SemaphoreType.DMA
    params = functools.partial(pltpu.CompilerParams, vmem_limit_bytes=24 << 20)
    rows = rows.T
    rows, counts, blocks, sketch = (
        pltpu.with_memory_space_constraint(a, pltpu.HBM) for a in (rows, counts, blocks, sketch)
    )
    terms = pl.pallas_call(
        terms_kernel,
        name="terms",
        out_shape=jax.ShapeDtypeStruct((feature_blocks,) + square, F32),
        in_specs=[hbm()] * 4,
        out_specs=vmem(),
        scratch_shapes=[
            pltpu.VMEM(blocks.shape, BF16), pltpu.VMEM(sketch.shape, BF16), dma((2, 4)),
            pltpu.SMEM(rows.shape, jnp.int32), pltpu.SMEM(counts.shape, jnp.int32), dma((2,)),
        ],
        compiler_params=params(),
    )(rows, counts, blocks, sketch)
    w = weights.reshape(feature_blocks, width)
    grid = (NY, NZ, NX, NC, PIECE, columns)
    streamed = (NZ // QZ, NC, 4, 4, QZ, PIECE, columns)
    gathered, summed, gram, turned = pl.pallas_call(
        exchange_kernel,
        name="exchange",
        out_shape=(
            jax.ShapeDtypeStruct(streamed, BF16), jax.ShapeDtypeStruct(tail, F32),
            jax.ShapeDtypeStruct(square, F32),
            jax.ShapeDtypeStruct((docs, width, slots * width), BF16),
        ),
        in_specs=[vmem(), vmem(), hbm()],
        out_specs=(vmem(), vmem(), vmem(), vmem()),
        scratch_shapes=[
            pltpu.VMEM(blocks.shape, BF16), dma(()), pltpu.VMEM(streamed, F32),
            pltpu.VMEM((16, 4, QZ) + tail, BF16), pltpu.VMEM((16, 4, QZ) + tail, BF16),
            pltpu.VMEM((12, 4, QZ) + tail, BF16), pltpu.VMEM((12, 4, QZ) + tail, BF16),
            pltpu.VMEM((12, QZ) + tail, BF16), pltpu.VMEM((12, QZ) + tail, BF16),
            pltpu.VMEM((NZ,) + tail, F32), pltpu.VMEM((NZ,) + tail, F32),
            pltpu.VMEM(square, F32),
            dma((2, 16)), dma((2, 12)), dma((2, 12)), dma((2, NZ)),
            dma((2, NZ)), dma((2, 12)), dma((2, 12)), dma((2, 16)),
        ],
        compiler_params=params(collective_id=0, has_side_effects=True),
    )(terms.reshape(grid), w, blocks)
    return pl.pallas_call(
        tail_kernel,
        name="tail",
        out_shape=(
            jax.ShapeDtypeStruct(tail, F32),
            jax.ShapeDtypeStruct((docs * width, columns), BF16),
        ),
        in_specs=[hbm(), hbm(), vmem(), vmem(), vmem(), vmem()],
        out_specs=(hbm(), hbm()),
        scratch_shapes=[
            pltpu.VMEM(square, F32), pltpu.VMEM(square, F32),
            pltpu.VMEM((docs,) + square, F32),
            pltpu.VMEM((docs * width, columns), BF16), pltpu.VMEM(tail, F32), dma((docs // 4 + 1,)),
            pltpu.SMEM(rows.shape, jnp.int32), pltpu.SMEM(counts.shape, jnp.int32), dma((2,)),
        ],
        compiler_params=params(),
    )(rows, counts, gathered, turned, gram, summed)


def solution(mesh):
    placed = (
        P(("row", "col"), None, None, None),
        P(("row", "col"), None),
        P(("row", "col")),
        P(("row", "col"), None),
        P(),
    )
    return jax.shard_map(
        body,
        mesh=mesh,
        in_specs=placed,
        out_specs=(P(("row", "col"), None), P(("row", "col"), None)),
        check_vma=False,
    )
```

```python
import functools

import jax
import jax.numpy as jnp
from jax import lax
from jax.experimental import pallas as pl
from jax.experimental.pallas import tpu as pltpu
from jax.sharding import PartitionSpec as P

HIGHEST = lax.Precision.HIGHEST
MESH = pl.DeviceIdType.MESH
F32, BF16 = jnp.float32, jnp.bfloat16
NX, NY, NZ, NC = 4, 4, 8, 2
QZ = 2
PIECE = 32
PANEL = 16


def scalars(rows_hbm, counts_hbm, rows_ref, counts_ref, sems):
    copies = [
        pltpu.make_async_copy(rows_hbm, rows_ref, sems.at[0]),
        pltpu.make_async_copy(counts_hbm, counts_ref, sems.at[1]),
    ]
    for copy in copies:
        copy.start()
    return copies


def terms_kernel(
    rows_hbm, counts_hbm, blocks_ref, sketch_ref, acc_ref,
    held, docs_held, sems, rows_ref, counts_ref, sem_i,
):
    docs, slots, width = held.shape[:3]
    step = 8
    indices = scalars(rows_hbm, counts_hbm, rows_ref, counts_ref, sem_i)
    copies = []
    for i in range(docs // step):
        a = pltpu.make_async_copy(sketch_ref.at[pl.ds(i * step * width, step * width)], docs_held.at[pl.ds(i * step * width, step * width)], sems.at[0, i])
        c = pltpu.make_async_copy(blocks_ref.at[pl.ds(i * step, step)], held.at[pl.ds(i * step, step)], sems.at[1, i])
        a.start()
        c.start()
        copies.append((a, c))
    zero = jnp.zeros((8, width, width), F32)

    def clear(i, carry):
        acc_ref[pl.ds(i * 8, 8)] = zero
        return carry

    lax.fori_loop(0, acc_ref.shape[0] // 8, clear, 0)
    for copy in indices:
        copy.wait()
    for d in range(docs):
        if d % step == 0:
            for copy in copies[d // step]:
                copy.wait()
        product = jnp.dot(
            held[d].reshape(slots * width, width),
            docs_held[d * width : (d + 1) * width, :],
            preferred_element_type=F32,
        )
        for s in range(slots):
            part = product[s * width : (s + 1) * width]
            used = s < counts_ref[d]
            acc_ref[rows_ref[s, d]] += jnp.where(used, part, jnp.zeros_like(part))


def exchange_kernel(
    p_ref, w_ref, blocks_ref, y_ref, s_ref, g_ref, bt_ref,
    held, sem_h, iw_ref, cs, cr, xs, xr, ys, yr, zs, zr, wide,
    sem0, sem_a, sem_b, sem_z, sem_gz, sem_gb, sem_ga, sem_p,
):
    row, col = lax.axis_index("row"), lax.axis_index("col")
    x, c = lax.div(col, NC), lax.rem(col, NC)
    y, z = lax.div(row, NZ), lax.rem(row, NZ)
    partner = (row, x * NC + (1 - c))

    def shift(v, k, n):
        return lax.rem(v + k, n)

    def at(xx, yy, zz):
        return (yy * NZ + zz, xx * NC + c)

    x_peer = [at(shift(x, k, NX), y, z) for k in range(NX)]
    y_peer = [at(x, shift(y, k, NY), z) for k in range(NY)]
    z_peer = [at(x, y, shift(z, k, NZ)) for k in range(NZ)]
    greet = [z_peer[k] for k in (4, 3, 5, 2, 6)] + [x_peer[2], y_peer[2]]
    greet += [z_peer[1], z_peer[7], x_peer[1], x_peer[3], y_peer[1], y_peer[3], partner]
    barrier = pltpu.get_barrier_semaphore()
    for peer in greet:
        pl.semaphore_signal(barrier, inc=1, device_id=peer, device_id_type=MESH)

    load = pltpu.make_async_copy(blocks_ref, held, sem_h)
    load.start()

    streams = range(NZ // QZ)
    a_peer = [(x_peer, y_peer)[s % 2] for s in streams]
    b_peer = [(y_peer, x_peer)[s % 2] for s in streams]
    a_at = [(x, y)[s % 2] for s in streams]
    b_at = [(y, x)[s % 2] for s in streams]
    started = []

    def copy_to(src, dst, send_sem, recv_sem, peer):
        return pltpu.make_async_remote_copy(
            src_ref=src, dst_ref=dst, send_sem=send_sem, recv_sem=recv_sem,
            device_id=peer, device_id_type=MESH,
        )

    def send(src, dst, sems, i, peer):
        copy = copy_to(src, dst, sems.at[0, i], sems.at[1, i], peer)
        copy.start()
        started.append(copy)
        return copy

    def piece(s, k, b, j, core):
        a = shift(a_at[s], k, 4)
        if s % 2 == 0:
            return (b, s * QZ + j, a, core)
        return (a, s * QZ + j, b, core)

    def inverse_weights(first, last):
        def some(i, carry):
            for j in range(8):
                w = w_ref[pl.ds(i * 8 + j, 1), :]
                turned = jnp.broadcast_to(1.0 / (w * w), wide.shape).T
                s, odd = lax.rem(i, 2) * 2 + j // 4, (j // 4) % 2
                for m in range(4):
                    ax = (lax.div(i, 2), 2 * (j % 2) + m // 2)
                    rows = turned[m * PIECE : (m + 1) * PIECE]
                    iw_ref[s, m % 2, ax[1 - odd], ax[odd], (j // 2) % 2] = rows
            return carry

        lax.fori_loop(first, last, some, 0)

    def turn_tiles(first, last):
        def some(i, carry):
            for j in range(4):
                d = i * 4 + j
                parts = [held[d, m].T for m in range(held.shape[1])]
                bt_ref[d] = jnp.concatenate(parts, axis=1)
            return carry

        lax.fori_loop(first, last, some, 0)

    def add_gram(s, core):
        tall = (4 * 4 * QZ * PIECE, wide.shape[1])
        part = y_ref[s, core].reshape(tall)
        scaled = (part.astype(F32) * iw_ref[s, core].reshape(tall)).astype(BF16)
        g_ref[...] += lax.dot_general(
            scaled, part, (((0,), (0,)), ((), ())), preferred_element_type=F32
        )

    for s, k in [(s, k) for s in streams for k in range(4)]:
        def fill(b, carry, s=s, k=k):
            for j in range(QZ):
                cs[s * 4 + k, b, j] = p_ref[piece(s, k, b, j, 1 - c)].astype(BF16)
            return carry

        lax.fori_loop(0, 4, fill, 0)

    flat = row * (NX * NC) + col
    w_row = w_ref[pl.ds(lax.div(flat, 4), 1), :]
    wide[...] = jnp.broadcast_to(w_row, wide.shape).T
    pl.semaphore_wait(barrier, len(greet))

    first, second, third = {}, {}, {}
    for s in streams:
        four = pl.ds(s * 4, 4)
        first[s] = send(cs.at[four], cr.at[four], sem0, s, partner)
    for s, k in [(s, k) for s in streams for k in (2, 1, 3)]:
        if k == 2:
            first[s].wait_recv()
        n = s * 3 + k - 1

        def add(b, carry, s=s, k=k, n=n):
            for j in range(QZ):
                total = p_ref[piece(s, k, b, j, c)] + cr[s * 4 + k, b, j].astype(F32)
                xs[n, b, j] = total.astype(BF16)
            return carry

        lax.fori_loop(0, 4, add, 0)
        second[s, k] = send(xs.at[n], xr.at[n], sem_a, n, a_peer[s][k])

    inverse_weights(0, 2)
    for s in streams:
        for k in (1, 3, 2):
            second[s, k].wait_recv()
        for k in (2, 1, 3, 0):
            b = shift(b_at[s], k, 4)
            for j in range(QZ):
                total = p_ref[piece(s, 0, b, j, c)] + cr[s * 4, b, j].astype(F32)
                for m in range(3):
                    total = total + xr[s * 3 + m, b, j].astype(F32)
                if k > 0:
                    ys[s * 3 + k - 1, j] = total.astype(BF16)
                else:
                    zs[s * QZ + j] = total
            if k > 0:
                n = s * 3 + k - 1
                third[s, k] = send(ys.at[n], yr.at[n], sem_b, n, b_peer[s][k])

    def fourth(there):
        return copy_to(
            zs.at[there], zr.at[z], sem_z.at[0, there], sem_z.at[1, z], at(x, y, there)
        )

    def arrival(k):
        here = shift(z, k, NZ)
        return copy_to(zs.at[here], zr.at[here], sem_z.at[0, here], sem_z.at[1, here], z_peer[k])

    for s in streams:
        for k in (1, 3, 2):
            third[s, k].wait_recv()
        for j in range(QZ):
            total = zs[s * QZ + j]
            for m in range(3):
                total = total + yr[s * 3 + m, j].astype(F32)
            zs[s * QZ + j] = total
        for j in range(QZ):
            there = s * QZ + j

            @pl.when(z != there)
            def _(there=there):
                fourth(there).start()

    inverse_weights(2, 6)
    total = zs[z]
    for k in (1, 7, 2, 6, 3, 5, 4):
        arrival(k).wait_recv()
        total = total + zr[shift(z, k, NZ)]
    w = wide[pl.ds(pl.multiple_of(lax.rem(flat, 4) * PIECE, PIECE), PIECE), :]
    summed = total * w
    s_ref[...] = summed

    mine_s, odd = lax.div(z, QZ), lax.rem(lax.div(z, QZ), 2)
    mine_a, mine_b = x + odd * (y - x), y + odd * (x - y)
    y_ref[mine_s, c, mine_a, mine_b, lax.rem(z, QZ)] = (summed * w).astype(BF16)
    mine = y_ref.at[mine_s, c, mine_a, mine_b, lax.rem(z, QZ)]
    old = list(started)
    started.clear()
    for k in (4, 3, 5, 2, 6, 1, 7):
        copy = copy_to(mine, mine, sem_gz.at[0, k], sem_gz.at[1, z], z_peer[k])
        copy.start()
        started.append(copy)
    gb, ga, paired = {}, {}, []
    inverse_weights(6, 8)
    load.wait()
    turn_tiles(0, 4)
    g_ref[...] = jnp.zeros_like(g_ref)
    for copy in old:
        copy.wait_send()
    for k in range(1, NZ):
        arrival(k).wait_send()

    def pair(part):
        paired.append(send(part, part, sem_p, len(paired), partner))

    for s in streams:
        part = y_ref.at[s, c, a_at[s], b_at[s]]
        for j in range(QZ):
            there = s * QZ + j

            @pl.when(z != there)
            def _(there=there, j=j, part=part):
                copy_to(
                    part.at[j], part.at[j], sem_gz.at[0, 0], sem_gz.at[1, there], at(x, y, there)
                ).wait_recv()

        for k in (2, 1, 3):
            gb[s, k] = send(part, part, sem_gb, s * 3 + k - 1, b_peer[s][k])
    for s in streams:
        for k in (1, 3, 2):
            gb[s, k].wait_recv()
        part = y_ref.at[s, c, a_at[s]]
        for k in (2, 1, 3):
            ga[s, k] = send(part, part, sem_ga, s * 3 + k - 1, a_peer[s][k])
    last = list(ga.values())
    for copy in started[: -len(last)]:
        copy.wait_send()

    def add_partner(s):
        paired[s].wait_recv()
        add_gram(s, 1 - c)

    for s in streams:
        for k in (1, 3, 2):
            ga[s, k].wait_recv()
        pair(y_ref.at[s, c])
        if s > 0:
            add_gram(s - 1, c)
        if s > 1:
            add_partner(s - 2)
    add_gram(streams[-1], c)
    for copy in last:
        copy.wait_send()
    for s in streams[-2:]:
        add_partner(s)
    for copy in paired:
        copy.wait_send()


def split(a):
    high = a.astype(BF16)
    return high, (a - high.astype(F32)).astype(BF16)


def factor(m_ref, linv_ref, b, between):
    n = m_ref.shape[0]
    whole = m_ref[...]
    on_diagonal = lax.broadcasted_iota(jnp.int32, (n, n), 0) == lax.broadcasted_iota(
        jnp.int32, (n, n), 1
    )
    diagonal = jnp.where(on_diagonal, whole, 0.0)
    across = lax.rsqrt(jnp.sum(diagonal, axis=0, keepdims=True))
    down = lax.rsqrt(jnp.sum(diagonal, axis=1, keepdims=True))
    m_ref[...] = whole * down * across
    lane = lax.broadcasted_iota(jnp.int32, (b, n), 1)
    sub = lax.broadcasted_iota(jnp.int32, (b, n), 0)
    for r0 in range(0, n, b):
        panel = m_ref[r0 : r0 + b, :]
        cols = jnp.stack(
            [jnp.broadcast_to(panel[:, r0 + j : r0 + j + 1], (b, n)) for j in range(b)]
        )
        inside = (lane >= r0) & (lane < r0 + b)
        panel = jnp.where(inside, (lane - r0 == sub).astype(F32), panel)
        pivots = jnp.ones((b, n), F32)
        for k in range(0, b, 2):
            base = (k // 8) * 8
            i = k - base
            c0, c1 = cols[0], cols[1]
            p, q, r = c0[i : i + 1], c1[i : i + 1], c1[i + 1 : i + 2]
            det = p * r - q * q
            over_p, over_det = 1.0 / p, 1.0 / det
            pivots = jnp.where(sub == k, p, jnp.where(sub == k + 1, det * over_p, pivots))
            below = sub[base:]
            alpha = jnp.where(
                below > k + 1,
                (r * c0 - q * c1) * over_det,
                jnp.where(below == k + 1, q * over_p, 0.0),
            )
            beta = jnp.where(below > k + 1, (p * c1 - q * c0) * over_det, 0.0)
            lower = panel[base:] - (alpha * panel[k : k + 1] + beta * panel[k + 1 : k + 2])
            panel = lower if base == 0 else jnp.concatenate([panel[:base], lower], axis=0)
            if k + 2 < b:
                rest = cols[2:]
                cols = rest - (
                    alpha[None] * rest[:, i : i + 1, :] + beta[None] * rest[:, i + 1 : i + 2, :]
                )
                if (k + 2) % 8 == 0:
                    cols = cols[:, 8:]
        scaled = panel * lax.rsqrt(pivots)
        linv_ref[r0 : r0 + b, :] = jnp.where(lane < r0 + b, scaled * across, 0.0)
        if r0 + b < n:
            h = scaled.astype(BF16)
            rem = scaled - h.astype(F32)
            m = rem.astype(BF16)
            l = (rem - m.astype(F32)).astype(BF16)
            right = lane >= r0 + b
            hf, mf, lf = (jnp.where(right, v.astype(F32), 0.0).astype(BF16) for v in (h, m, l))
            update = lax.dot_general(
                jnp.concatenate([hf, hf, mf, mf, hf, lf], axis=0),
                jnp.concatenate([h, m, h, m, l, h], axis=0),
                (((0,), (0,)), ((), ())),
                preferred_element_type=F32,
            )
            rest = m_ref[r0 + b :, :]
            lane2 = lax.broadcasted_iota(jnp.int32, rest.shape, 1)
            rest = jnp.where((lane2 >= r0) & (lane2 < r0 + b), 0.0, rest)
            m_ref[r0 + b :, :] = rest - update[r0 + b :, :]
        between(r0 // b)


def tail_kernel(
    rows_hbm, counts_hbm, y_ref, bt_ref, g_ref, s_ref, basis_ref, factors_ref,
    m_ref, linv_ref, t_ref, f_ref, b_ref, sem_o, rows_ref, counts_ref, sem_i,
):
    slots, docs = rows_ref.shape
    width = g_ref.shape[0]
    features = y_ref.size // width
    indices = scalars(rows_hbm, counts_hbm, rows_ref, counts_ref, sem_i)
    m_ref[...] = g_ref[...] * (1.0 / features)

    def tile(f):
        row = lax.div(f, 2)
        y, z = lax.div(row, NZ), lax.rem(row, NZ)
        s = lax.div(z, QZ)
        odd = lax.rem(s, 2)
        parts = []
        for m in range(4):
            x = lax.rem(f, 2) * 2 + m // 2
            a, b = x + odd * (y - x), y + odd * (x - y)
            parts.append(y_ref[s, m % 2, a, b, lax.rem(z, QZ)])
        return jnp.concatenate(parts, axis=0)

    def product(d):
        parts = []
        for s in range(slots):
            part = tile(rows_ref[s, d])
            parts.append(jnp.where(s < counts_ref[d], part, jnp.zeros_like(part)))
        t_ref[d] = jnp.dot(bt_ref[d], jnp.concatenate(parts, axis=0), preferred_element_type=F32)

    panels = width // PANEL

    def between(panel):
        if panel == 0:
            for copy in indices:
                copy.wait()
        last = docs * (panel + 1) // panels
        for d in range(docs * panel // panels, last):
            product(d)

    factor(m_ref, linv_ref, PANEL, between)
    inverse = linv_ref[...]
    high, low = split(inverse)
    left = jnp.concatenate([high, low], axis=0)
    right = jnp.concatenate([high, jnp.zeros_like(low)], axis=0)
    both = jnp.concatenate([left, right], axis=1)
    copies = []

    def put(src, dst):
        copy = pltpu.make_async_copy(src, dst, sem_o.at[len(copies)])
        copy.start()
        copies.append(copy)

    for d in range(docs):
        t_high, t_low = split(t_ref[d])
        out = lax.dot_general(
            jnp.concatenate([t_high, t_low], axis=1), both,
            (((1,), (1,)), ((), ())), preferred_element_type=F32,
        )
        rows = pl.ds(d * width, width)
        f_ref[rows, :] = (out[:, :width] + out[:, width:]).astype(BF16)
        if d % 4 == 3:
            rows = pl.ds((d - 3) * width, 4 * width)
            put(f_ref.at[rows], factors_ref.at[rows])
        if d == 0:
            b_ref[...] = lax.dot_general(
                s_ref[...], inverse, (((1,), (1,)), ((), ())),
                precision=HIGHEST, preferred_element_type=F32,
            )
            put(b_ref, basis_ref)
    for copy in copies:
        copy.wait()


def vmem():
    return pl.BlockSpec(memory_space=pltpu.VMEM)


def hbm():
    return pl.BlockSpec(memory_space=pltpu.HBM)


def body(blocks, rows, counts, sketch, weights):
    docs, slots, width = blocks.shape[:3]
    features = weights.shape[0]
    feature_blocks = features // width
    columns = sketch.shape[1]
    square = (width, columns)
    tail = (PIECE, columns)
    dma = pltpu.SemaphoreType.DMA
    params = functools.partial(pltpu.CompilerParams, vmem_limit_bytes=24 << 20)
    rows = rows.T
    rows, counts, blocks, sketch = (
        pltpu.with_memory_space_constraint(a, pltpu.HBM) for a in (rows, counts, blocks, sketch)
    )
    terms = pl.pallas_call(
        terms_kernel,
        name="terms",
        out_shape=jax.ShapeDtypeStruct((feature_blocks,) + square, F32),
        in_specs=[hbm()] * 4,
        out_specs=vmem(),
        scratch_shapes=[
            pltpu.VMEM(blocks.shape, BF16), pltpu.VMEM(sketch.shape, BF16), dma((2, 2)),
            pltpu.SMEM(rows.shape, jnp.int32), pltpu.SMEM(counts.shape, jnp.int32), dma((2,)),
        ],
        compiler_params=params(),
    )(rows, counts, blocks, sketch)
    w = weights.reshape(feature_blocks, width)
    grid = (NY, NZ, NX, NC, PIECE, columns)
    streamed = (NZ // QZ, NC, 4, 4, QZ, PIECE, columns)
    gathered, summed, gram, turned = pl.pallas_call(
        exchange_kernel,
        name="exchange",
        out_shape=(
            jax.ShapeDtypeStruct(streamed, BF16), jax.ShapeDtypeStruct(tail, F32),
            jax.ShapeDtypeStruct(square, F32),
            jax.ShapeDtypeStruct((docs, width, slots * width), BF16),
        ),
        in_specs=[vmem(), vmem(), hbm()],
        out_specs=(vmem(), vmem(), vmem(), vmem()),
        scratch_shapes=[
            pltpu.VMEM(blocks.shape, BF16), dma(()), pltpu.VMEM(streamed, F32),
            pltpu.VMEM((16, 4, QZ) + tail, BF16), pltpu.VMEM((16, 4, QZ) + tail, BF16),
            pltpu.VMEM((12, 4, QZ) + tail, BF16), pltpu.VMEM((12, 4, QZ) + tail, BF16),
            pltpu.VMEM((12, QZ) + tail, BF16), pltpu.VMEM((12, QZ) + tail, BF16),
            pltpu.VMEM((NZ,) + tail, F32), pltpu.VMEM((NZ,) + tail, F32),
            pltpu.VMEM(square, F32),
            dma((2, 4)), dma((2, 12)), dma((2, 12)), dma((2, NZ)),
            dma((2, NZ)), dma((2, 12)), dma((2, 12)), dma((2, 4)),
        ],
        compiler_params=params(collective_id=0, has_side_effects=True),
    )(terms.reshape(grid), w, blocks)
    return pl.pallas_call(
        tail_kernel,
        name="tail",
        out_shape=(
            jax.ShapeDtypeStruct(tail, F32),
            jax.ShapeDtypeStruct((docs * width, columns), BF16),
        ),
        in_specs=[hbm(), hbm(), vmem(), vmem(), vmem(), vmem()],
        out_specs=(hbm(), hbm()),
        scratch_shapes=[
            pltpu.VMEM(square, F32), pltpu.VMEM(square, F32),
            pltpu.VMEM((docs,) + square, F32),
            pltpu.VMEM((docs * width, columns), BF16), pltpu.VMEM(tail, F32), dma((docs // 4 + 1,)),
            pltpu.SMEM(rows.shape, jnp.int32), pltpu.SMEM(counts.shape, jnp.int32), dma((2,)),
        ],
        compiler_params=params(),
    )(rows, counts, gathered, turned, gram, summed)


def solution(mesh):
    placed = (
        P(("row", "col"), None, None, None),
        P(("row", "col"), None),
        P(("row", "col")),
        P(("row", "col"), None),
        P(),
    )
    return jax.shard_map(
        body,
        mesh=mesh,
        in_specs=placed,
        out_specs=(P(("row", "col"), None), P(("row", "col"), None)),
        check_vma=False,
    )
```

```python
import functools

import jax
import jax.numpy as jnp
from jax import lax
from jax.experimental import pallas as pl
from jax.experimental.pallas import tpu as pltpu
from jax.sharding import PartitionSpec as P

HIGHEST = lax.Precision.HIGHEST
MESH = pl.DeviceIdType.MESH
F32, BF16 = jnp.float32, jnp.bfloat16
NX, NY, NZ, NC = 4, 4, 8, 2
QZ = 2
PIECE = 32
PANEL = 16


def scalars(rows_hbm, counts_hbm, rows_ref, counts_ref, sems):
    copies = [
        pltpu.make_async_copy(rows_hbm, rows_ref, sems.at[0]),
        pltpu.make_async_copy(counts_hbm, counts_ref, sems.at[1]),
    ]
    for copy in copies:
        copy.start()
    return copies


def terms_kernel(
    rows_hbm, counts_hbm, blocks_ref, sketch_ref, acc_ref,
    held, docs_held, sems, rows_ref, counts_ref, sem_i,
):
    docs, slots, width = held.shape[:3]
    step = 8
    indices = scalars(rows_hbm, counts_hbm, rows_ref, counts_ref, sem_i)
    copies = []
    for i in range(docs // step):
        a = pltpu.make_async_copy(sketch_ref.at[pl.ds(i * step * width, step * width)], docs_held.at[pl.ds(i * step * width, step * width)], sems.at[0, i])
        c = pltpu.make_async_copy(blocks_ref.at[pl.ds(i * step, step)], held.at[pl.ds(i * step, step)], sems.at[1, i])
        a.start()
        c.start()
        copies.append((a, c))
    zero = jnp.zeros((8, width, width), F32)

    def clear(i, carry):
        acc_ref[pl.ds(i * 8, 8)] = zero
        return carry

    lax.fori_loop(0, acc_ref.shape[0] // 8, clear, 0)
    for copy in indices:
        copy.wait()
    for d in range(docs):
        if d % step == 0:
            for copy in copies[d // step]:
                copy.wait()
        product = jnp.dot(
            held[d].reshape(slots * width, width),
            docs_held[d * width : (d + 1) * width, :],
            preferred_element_type=F32,
        )
        for s in range(slots):
            part = product[s * width : (s + 1) * width]
            used = s < counts_ref[d]
            acc_ref[rows_ref[s, d]] += jnp.where(used, part, jnp.zeros_like(part))


def exchange_kernel(
    p_ref, w_ref, blocks_ref, y_ref, s_ref, g_ref, bt_ref,
    held, sem_h, iw_ref, cs, cr, xs, xr, ys, yr, zs, zr, wide,
    sem0, sem_a, sem_b, sem_z, sem_gz, sem_gb, sem_ga, sem_p,
):
    row, col = lax.axis_index("row"), lax.axis_index("col")
    x, c = lax.div(col, NC), lax.rem(col, NC)
    y, z = lax.div(row, NZ), lax.rem(row, NZ)
    partner = (row, x * NC + (1 - c))

    def shift(v, k, n):
        return lax.rem(v + k, n)

    def at(xx, yy, zz):
        return (yy * NZ + zz, xx * NC + c)

    x_peer = [at(shift(x, k, NX), y, z) for k in range(NX)]
    y_peer = [at(x, shift(y, k, NY), z) for k in range(NY)]
    z_peer = [at(x, y, shift(z, k, NZ)) for k in range(NZ)]
    greet = [z_peer[k] for k in (4, 3, 5, 2, 6)] + [x_peer[2], y_peer[2]]
    greet += [z_peer[1], z_peer[7], x_peer[1], x_peer[3], y_peer[1], y_peer[3], partner]
    barrier = pltpu.get_barrier_semaphore()
    for peer in greet:
        pl.semaphore_signal(barrier, inc=1, device_id=peer, device_id_type=MESH)

    load = pltpu.make_async_copy(blocks_ref, held, sem_h)
    load.start()

    streams = range(NZ // QZ)
    a_peer = [(x_peer, y_peer)[s % 2] for s in streams]
    b_peer = [(y_peer, x_peer)[s % 2] for s in streams]
    a_at = [(x, y)[s % 2] for s in streams]
    b_at = [(y, x)[s % 2] for s in streams]
    started = []

    def copy_to(src, dst, send_sem, recv_sem, peer):
        return pltpu.make_async_remote_copy(
            src_ref=src, dst_ref=dst, send_sem=send_sem, recv_sem=recv_sem,
            device_id=peer, device_id_type=MESH,
        )

    def send(src, dst, sems, i, peer):
        copy = copy_to(src, dst, sems.at[0, i], sems.at[1, i], peer)
        copy.start()
        started.append(copy)
        return copy

    def piece(s, k, b, j, core):
        a = shift(a_at[s], k, 4)
        if s % 2 == 0:
            return (b, s * QZ + j, a, core)
        return (a, s * QZ + j, b, core)

    def inverse_weights(first, last):
        def some(i, carry):
            for j in range(8):
                w = w_ref[pl.ds(i * 8 + j, 1), :]
                turned = jnp.broadcast_to(1.0 / (w * w), wide.shape).T
                s, odd = lax.rem(i, 2) * 2 + j // 4, (j // 4) % 2
                for m in range(4):
                    ax = (lax.div(i, 2), 2 * (j % 2) + m // 2)
                    rows = turned[m * PIECE : (m + 1) * PIECE]
                    iw_ref[s, m % 2, ax[1 - odd], ax[odd], (j // 2) % 2] = rows
            return carry

        lax.fori_loop(first, last, some, 0)

    def turn_tiles(first, last):
        def some(i, carry):
            for j in range(4):
                d = i * 4 + j
                parts = [held[d, m].T for m in range(held.shape[1])]
                bt_ref[d] = jnp.concatenate(parts, axis=1)
            return carry

        lax.fori_loop(first, last, some, 0)

    def add_gram(s, core):
        tall = (4 * 4 * QZ * PIECE, wide.shape[1])
        part = y_ref[s, core].reshape(tall)
        scaled = (part.astype(F32) * iw_ref[s, core].reshape(tall)).astype(BF16)
        g_ref[...] += lax.dot_general(
            scaled, part, (((0,), (0,)), ((), ())), preferred_element_type=F32
        )

    for s, k in [(s, k) for s in streams for k in range(4)]:
        def fill(b, carry, s=s, k=k):
            for j in range(QZ):
                cs[s * 4 + k, b, j] = p_ref[piece(s, k, b, j, 1 - c)].astype(BF16)
            return carry

        lax.fori_loop(0, 4, fill, 0)

    flat = row * (NX * NC) + col
    w_row = w_ref[pl.ds(lax.div(flat, 4), 1), :]
    wide[...] = jnp.broadcast_to(w_row, wide.shape).T
    pl.semaphore_wait(barrier, len(greet))

    first, second, third = {}, {}, {}
    for s in streams:
        four = pl.ds(s * 4, 4)
        first[s] = send(cs.at[four], cr.at[four], sem0, s, partner)
    for s, k in [(s, k) for s in streams for k in (2, 1, 3)]:
        if k == 2:
            first[s].wait_recv()
        n = s * 3 + k - 1

        for b in range(4):
            for j in range(QZ):
                total = p_ref[piece(s, k, b, j, c)] + cr[s * 4 + k, b, j].astype(F32)
                xs[n, b, j] = total.astype(BF16)
        second[s, k] = send(xs.at[n], xr.at[n], sem_a, n, a_peer[s][k])

    for s in streams:
        for k in (1, 3, 2):
            second[s, k].wait_recv()
        for k in (2, 1, 3, 0):
            b = shift(b_at[s], k, 4)
            for j in range(QZ):
                total = p_ref[piece(s, 0, b, j, c)] + cr[s * 4, b, j].astype(F32)
                for m in range(3):
                    total = total + xr[s * 3 + m, b, j].astype(F32)
                if k > 0:
                    ys[s * 3 + k - 1, j] = total.astype(BF16)
                else:
                    zs[s * QZ + j] = total
            if k > 0:
                n = s * 3 + k - 1
                third[s, k] = send(ys.at[n], yr.at[n], sem_b, n, b_peer[s][k])

    def fourth(there):
        return copy_to(
            zs.at[there], zr.at[z], sem_z.at[0, there], sem_z.at[1, z], at(x, y, there)
        )

    def arrival(k):
        here = shift(z, k, NZ)
        return copy_to(zs.at[here], zr.at[here], sem_z.at[0, here], sem_z.at[1, here], z_peer[k])

    inverse_weights(0, 2)
    for s in streams:
        for k in (1, 3, 2):
            third[s, k].wait_recv()
        for j in range(QZ):
            total = zs[s * QZ + j]
            for m in range(3):
                total = total + yr[s * 3 + m, j].astype(F32)
            zs[s * QZ + j] = total
        for j in range(QZ):
            there = s * QZ + j

            @pl.when(z != there)
            def _(there=there):
                fourth(there).start()

    inverse_weights(2, 6)
    total = zs[z]
    for k in (1, 7, 2, 6, 3, 5, 4):
        arrival(k).wait_recv()
        total = total + zr[shift(z, k, NZ)]
    w = wide[pl.ds(pl.multiple_of(lax.rem(flat, 4) * PIECE, PIECE), PIECE), :]
    summed = total * w
    s_ref[...] = summed

    mine_s, odd = lax.div(z, QZ), lax.rem(lax.div(z, QZ), 2)
    mine_a, mine_b = x + odd * (y - x), y + odd * (x - y)
    y_ref[mine_s, c, mine_a, mine_b, lax.rem(z, QZ)] = (summed * w).astype(BF16)
    mine = y_ref.at[mine_s, c, mine_a, mine_b, lax.rem(z, QZ)]
    old = list(started)
    started.clear()
    for k in (4, 3, 5, 2, 6, 1, 7):
        copy = copy_to(mine, mine, sem_gz.at[0, k], sem_gz.at[1, z], z_peer[k])
        copy.start()
        started.append(copy)
    gb, ga, paired = {}, {}, []
    inverse_weights(6, 8)
    load.wait()
    turn_tiles(0, 4)
    g_ref[...] = jnp.zeros_like(g_ref)
    for copy in old:
        copy.wait_send()
    for k in range(1, NZ):
        arrival(k).wait_send()

    def pair(part):
        paired.append(send(part, part, sem_p, len(paired), partner))

    for s in streams:
        part = y_ref.at[s, c, a_at[s], b_at[s]]
        for j in range(QZ):
            there = s * QZ + j

            @pl.when(z != there)
            def _(there=there, j=j, part=part):
                copy_to(
                    part.at[j], part.at[j], sem_gz.at[0, 0], sem_gz.at[1, there], at(x, y, there)
                ).wait_recv()

        for k in (2, 1, 3):
            gb[s, k] = send(part, part, sem_gb, s * 3 + k - 1, b_peer[s][k])
    for s in streams:
        for k in (1, 3, 2):
            gb[s, k].wait_recv()
        part = y_ref.at[s, c, a_at[s]]
        for k in (2, 1, 3):
            ga[s, k] = send(part, part, sem_ga, s * 3 + k - 1, a_peer[s][k])
    last = list(ga.values())
    for copy in started[: -len(last)]:
        copy.wait_send()

    def add_partner(s):
        paired[s].wait_recv()
        add_gram(s, 1 - c)

    for s in streams:
        for k in (1, 3, 2):
            ga[s, k].wait_recv()
        pair(y_ref.at[s, c])
        if s > 0:
            add_gram(s - 1, c)
        if s > 1:
            add_partner(s - 2)
    add_gram(streams[-1], c)
    for copy in last:
        copy.wait_send()
    for s in streams[-2:]:
        add_partner(s)
    for copy in paired:
        copy.wait_send()


def split(a):
    high = a.astype(BF16)
    return high, (a - high.astype(F32)).astype(BF16)


def factor(m_ref, linv_ref, b, between):
    n = m_ref.shape[0]
    whole = m_ref[...]
    on_diagonal = lax.broadcasted_iota(jnp.int32, (n, n), 0) == lax.broadcasted_iota(
        jnp.int32, (n, n), 1
    )
    diagonal = jnp.where(on_diagonal, whole, 0.0)
    across = lax.rsqrt(jnp.sum(diagonal, axis=0, keepdims=True))
    down = lax.rsqrt(jnp.sum(diagonal, axis=1, keepdims=True))
    m_ref[...] = whole * down * across
    lane = lax.broadcasted_iota(jnp.int32, (b, n), 1)
    sub = lax.broadcasted_iota(jnp.int32, (b, n), 0)
    for r0 in range(0, n, b):
        panel = m_ref[r0 : r0 + b, :]
        cols = jnp.stack(
            [jnp.broadcast_to(panel[:, r0 + j : r0 + j + 1], (b, n)) for j in range(b)]
        )
        inside = (lane >= r0) & (lane < r0 + b)
        panel = jnp.where(inside, (lane - r0 == sub).astype(F32), panel)
        pivots = jnp.ones((b, n), F32)
        for k in range(0, b, 2):
            base = (k // 8) * 8
            i = k - base
            c0, c1 = cols[0], cols[1]
            p, q, r = c0[i : i + 1], c1[i : i + 1], c1[i + 1 : i + 2]
            det = p * r - q * q
            over_p, over_det = 1.0 / p, 1.0 / det
            pivots = jnp.where(sub == k, p, jnp.where(sub == k + 1, det * over_p, pivots))
            below = sub[base:]
            alpha = jnp.where(
                below > k + 1,
                (r * c0 - q * c1) * over_det,
                jnp.where(below == k + 1, q * over_p, 0.0),
            )
            beta = jnp.where(below > k + 1, (p * c1 - q * c0) * over_det, 0.0)
            lower = panel[base:] - (alpha * panel[k : k + 1] + beta * panel[k + 1 : k + 2])
            panel = lower if base == 0 else jnp.concatenate([panel[:base], lower], axis=0)
            if k + 2 < b:
                rest = cols[2:]
                cols = rest - (
                    alpha[None] * rest[:, i : i + 1, :] + beta[None] * rest[:, i + 1 : i + 2, :]
                )
                if (k + 2) % 8 == 0:
                    cols = cols[:, 8:]
        scaled = panel * lax.rsqrt(pivots)
        linv_ref[r0 : r0 + b, :] = jnp.where(lane < r0 + b, scaled * across, 0.0)
        if r0 + b < n:
            h = scaled.astype(BF16)
            rem = scaled - h.astype(F32)
            m = rem.astype(BF16)
            l = (rem - m.astype(F32)).astype(BF16)
            right = lane >= r0 + b
            hf, mf, lf = (jnp.where(right, v.astype(F32), 0.0).astype(BF16) for v in (h, m, l))
            update = lax.dot_general(
                jnp.concatenate([hf, hf, mf, mf, hf, lf], axis=0),
                jnp.concatenate([h, m, h, m, l, h], axis=0),
                (((0,), (0,)), ((), ())),
                preferred_element_type=F32,
            )
            rest = m_ref[r0 + b :, :]
            lane2 = lax.broadcasted_iota(jnp.int32, rest.shape, 1)
            rest = jnp.where((lane2 >= r0) & (lane2 < r0 + b), 0.0, rest)
            m_ref[r0 + b :, :] = rest - update[r0 + b :, :]
        between(r0 // b)


def tail_kernel(
    rows_hbm, counts_hbm, y_ref, bt_ref, g_ref, s_ref, basis_ref, factors_ref,
    m_ref, linv_ref, t_ref, f_ref, b_ref, sem_o, rows_ref, counts_ref, sem_i,
):
    slots, docs = rows_ref.shape
    width = g_ref.shape[0]
    features = y_ref.size // width
    indices = scalars(rows_hbm, counts_hbm, rows_ref, counts_ref, sem_i)
    m_ref[...] = g_ref[...] * (1.0 / features)

    def tile(f):
        row = lax.div(f, 2)
        y, z = lax.div(row, NZ), lax.rem(row, NZ)
        s = lax.div(z, QZ)
        odd = lax.rem(s, 2)
        parts = []
        for m in range(4):
            x = lax.rem(f, 2) * 2 + m // 2
            a, b = x + odd * (y - x), y + odd * (x - y)
            parts.append(y_ref[s, m % 2, a, b, lax.rem(z, QZ)])
        return jnp.concatenate(parts, axis=0)

    def product(d):
        parts = []
        for s in range(slots):
            part = tile(rows_ref[s, d])
            parts.append(jnp.where(s < counts_ref[d], part, jnp.zeros_like(part)))
        t_ref[d] = jnp.dot(bt_ref[d], jnp.concatenate(parts, axis=0), preferred_element_type=F32)

    panels = width // PANEL

    def between(panel):
        if panel == 0:
            for copy in indices:
                copy.wait()
        last = docs * (panel + 1) // panels
        for d in range(docs * panel // panels, last):
            product(d)

    factor(m_ref, linv_ref, PANEL, between)
    inverse = linv_ref[...]
    high, low = split(inverse)
    left = jnp.concatenate([high, low], axis=0)
    right = jnp.concatenate([high, jnp.zeros_like(low)], axis=0)
    both = jnp.concatenate([left, right], axis=1)
    copies = []

    def put(src, dst):
        copy = pltpu.make_async_copy(src, dst, sem_o.at[len(copies)])
        copy.start()
        copies.append(copy)

    for d in range(docs):
        t_high, t_low = split(t_ref[d])
        out = lax.dot_general(
            jnp.concatenate([t_high, t_low], axis=1), both,
            (((1,), (1,)), ((), ())), preferred_element_type=F32,
        )
        rows = pl.ds(d * width, width)
        f_ref[rows, :] = (out[:, :width] + out[:, width:]).astype(BF16)
        if d % 4 == 3:
            rows = pl.ds((d - 3) * width, 4 * width)
            put(f_ref.at[rows], factors_ref.at[rows])
        if d == 0:
            b_ref[...] = lax.dot_general(
                s_ref[...], inverse, (((1,), (1,)), ((), ())),
                precision=HIGHEST, preferred_element_type=F32,
            )
            put(b_ref, basis_ref)
    for copy in copies:
        copy.wait()


def vmem():
    return pl.BlockSpec(memory_space=pltpu.VMEM)


def hbm():
    return pl.BlockSpec(memory_space=pltpu.HBM)


def body(blocks, rows, counts, sketch, weights):
    docs, slots, width = blocks.shape[:3]
    features = weights.shape[0]
    feature_blocks = features // width
    columns = sketch.shape[1]
    square = (width, columns)
    tail = (PIECE, columns)
    dma = pltpu.SemaphoreType.DMA
    params = functools.partial(pltpu.CompilerParams, vmem_limit_bytes=24 << 20)
    rows = rows.T
    rows, counts, blocks, sketch = (
        pltpu.with_memory_space_constraint(a, pltpu.HBM) for a in (rows, counts, blocks, sketch)
    )
    terms = pl.pallas_call(
        terms_kernel,
        name="terms",
        out_shape=jax.ShapeDtypeStruct((feature_blocks,) + square, F32),
        in_specs=[hbm()] * 4,
        out_specs=vmem(),
        scratch_shapes=[
            pltpu.VMEM(blocks.shape, BF16), pltpu.VMEM(sketch.shape, BF16), dma((2, 2)),
            pltpu.SMEM(rows.shape, jnp.int32), pltpu.SMEM(counts.shape, jnp.int32), dma((2,)),
        ],
        compiler_params=params(),
    )(rows, counts, blocks, sketch)
    w = weights.reshape(feature_blocks, width)
    grid = (NY, NZ, NX, NC, PIECE, columns)
    streamed = (NZ // QZ, NC, 4, 4, QZ, PIECE, columns)
    gathered, summed, gram, turned = pl.pallas_call(
        exchange_kernel,
        name="exchange",
        out_shape=(
            jax.ShapeDtypeStruct(streamed, BF16), jax.ShapeDtypeStruct(tail, F32),
            jax.ShapeDtypeStruct(square, F32),
            jax.ShapeDtypeStruct((docs, width, slots * width), BF16),
        ),
        in_specs=[vmem(), vmem(), hbm()],
        out_specs=(vmem(), vmem(), vmem(), vmem()),
        scratch_shapes=[
            pltpu.VMEM(blocks.shape, BF16), dma(()), pltpu.VMEM(streamed, F32),
            pltpu.VMEM((16, 4, QZ) + tail, BF16), pltpu.VMEM((16, 4, QZ) + tail, BF16),
            pltpu.VMEM((12, 4, QZ) + tail, BF16), pltpu.VMEM((12, 4, QZ) + tail, BF16),
            pltpu.VMEM((12, QZ) + tail, BF16), pltpu.VMEM((12, QZ) + tail, BF16),
            pltpu.VMEM((NZ,) + tail, F32), pltpu.VMEM((NZ,) + tail, F32),
            pltpu.VMEM(square, F32),
            dma((2, 4)), dma((2, 12)), dma((2, 12)), dma((2, NZ)),
            dma((2, NZ)), dma((2, 12)), dma((2, 12)), dma((2, 4)),
        ],
        compiler_params=params(collective_id=0, has_side_effects=True),
    )(terms.reshape(grid), w, blocks)
    return pl.pallas_call(
        tail_kernel,
        name="tail",
        out_shape=(
            jax.ShapeDtypeStruct(tail, F32),
            jax.ShapeDtypeStruct((docs * width, columns), BF16),
        ),
        in_specs=[hbm(), hbm(), vmem(), vmem(), vmem(), vmem()],
        out_specs=(hbm(), hbm()),
        scratch_shapes=[
            pltpu.VMEM(square, F32), pltpu.VMEM(square, F32),
            pltpu.VMEM((docs,) + square, F32),
            pltpu.VMEM((docs * width, columns), BF16), pltpu.VMEM(tail, F32), dma((docs // 4 + 1,)),
            pltpu.SMEM(rows.shape, jnp.int32), pltpu.SMEM(counts.shape, jnp.int32), dma((2,)),
        ],
        compiler_params=params(),
    )(rows, counts, gathered, turned, gram, summed)


def solution(mesh):
    placed = (
        P(("row", "col"), None, None, None),
        P(("row", "col"), None),
        P(("row", "col")),
        P(("row", "col"), None),
        P(),
    )
    return jax.shard_map(
        body,
        mesh=mesh,
        in_specs=placed,
        out_specs=(P(("row", "col"), None), P(("row", "col"), None)),
        check_vma=False,
    )
```
